128 devices in a mesh: dom: 128 (over z, y, x, core).
Axes of the slice: x: 4, y: 4, z: 4, core: 2. Of those that a mesh axis runs over, the one named last changes fastest.
Arguments:
- solution: float32 [4, 20, 262144], P(None, None, 'dom'), may hold values from -6 to 6
- register: float32 [4, 20, 262144], P(None, None, 'dom'), may hold values from -4 to 4
- geometry: float32 [9, 262144], P(None, 'dom'), may hold values from -4 to 4
- normals: float32 [3, 4, 262144], P(None, None, 'dom'), may hold values from -1 to 1, as said below
- face_scale: float32 [4, 262144], P(None, 'dom'), may hold values from 0.5 to 2
- impedance: float32 [16], replicated, may hold values from 0.2 to 5
- neighbour: int32 [4, 262144], P(None, 'dom'), may hold values from -1 to 9215, as said below
- orientation: int32 [4, 262144], P(None, 'dom'), may hold values from 0 to 2
- wall_material: int32 [4, 262144], P(None, 'dom'), may hold values from 0 to 15
- send_faces: int32 [1024, 128], P('dom'), may hold values from -1 to 8191, as said below
Outputs:
- solution_next: float32 [4, 20, 262144], P(None, None, 'dom')
- register_next: float32 [4, 20, 262144], P(None, None, 'dom')
- absorbed: float32 [2, 16], replicated
The draws below stay inside these ranges and needn't reach their ends.
Inputs may be any that keep to these rules, and one draw needn't show every extreme that they name: `neighbour`: A value below 8192 names a face of the same partition, and that face names this one back; a larger value names a received slot as in the reference program, and the face in that slot names this face back in the same way; -1 marks a wall face. `send_faces`: row j of partition d lists distinct local faces (numbered f * 2048 + e) sent to partition d + o_j in slot order, then -1; rows for partitions outside the mesh are all -1; the lists of two partitions for each other have equal lengths, and at most 128 faces go from one partition to another, a bound that is reached. Each face's three entries form a unit vector, and two faces that name each other as neighbours have opposite normals.
All inputs are finite; a program needn't handle non-finite values.
Results may differ from the reference program's by a relative error of at most 0.0003.
Values sent between devices are 32-bit elements; how exact they have to be, the bound alone decides.
No kernel may reach another device: no remote copies, remote signals or barrier semaphores. Data moves between devices by JAX's collectives and lax.ppermute only.
A program may use at most 128 MiB of HBM per device.

```python
import math
import jax
import jax.numpy as jnp
from jax import lax

E_DEV = 2048
CAP = 128
NBR_HALF = 4
NMAT = 16
NODES = 20
ELEMS = 262144
N_DOM = 128


def peer_shift(index, half_span):
    return index - half_span if index < half_span else index - half_span + 1


def make_links(key):
    face_count = 4 * E_DEV
    half_span = NBR_HALF
    blocks = 2 * half_span
    pair_counts = jax.random.randint(jax.random.fold_in(key, 11), (N_DOM, half_span), CAP // 4, CAP + 1).astype(jnp.int32)
    pair_counts = pair_counts.at[0, 0].set(CAP)
    pair_counts = pair_counts.at[0, half_span - 1].set(CAP)
    device_ids = jnp.arange(N_DOM, dtype=jnp.int32)
    columns = []
    for j in range(blocks):
        offset = peer_shift(j, half_span)
        low_end = device_ids if offset > 0 else device_ids + offset
        inside = (device_ids + offset >= 0) & (device_ids + offset < N_DOM)
        counts = pair_counts[jnp.clip(low_end, 0, N_DOM - 1), abs(offset) - 1]
        columns.append(jnp.where(inside, counts, 0))
    block_counts = jnp.stack(columns, axis=1).astype(jnp.int32)
    extra_walls = jax.random.randint(jax.random.fold_in(key, 17), (N_DOM,), 0, face_count // 32 + 1).astype(jnp.int32)
    wall_counts = face_count * (N_DOM - 1 + 2 * device_ids) // (16 * (N_DOM - 1)) + extra_walls
    base_key = jax.random.fold_in(key, 23)
    device_keys = jax.vmap(lambda d: jax.random.fold_in(base_key, d))(device_ids)

    def per_device(device_key, counts, wall_count):
        shuffled = jax.random.permutation(device_key, face_count).astype(jnp.int32)
        starts = jnp.cumsum(counts) - counts
        slot_ids = jnp.arange(CAP, dtype=jnp.int32)
        in_use = slot_ids[None, :] < counts[:, None]
        chosen = shuffled[jnp.clip(starts[:, None] + slot_ids[None, :], 0, face_count - 1)]
        send_list = jnp.where(in_use, chosen, -1).astype(jnp.int32)
        slot_codes = face_count + jnp.arange(blocks, dtype=jnp.int32)[:, None] * CAP + slot_ids[None, :]
        link_table = jnp.full((face_count,), -1, jnp.int32)
        link_table = link_table.at[jnp.where(in_use, chosen, face_count).reshape(-1)].set(slot_codes.reshape(-1).astype(jnp.int32), mode='drop')
        used_faces = jnp.sum(counts) + wall_count
        pair_count = (face_count - used_faces) // 2
        pair_ids = jnp.arange(face_count // 2, dtype=jnp.int32)
        first_face = shuffled[jnp.clip(used_faces + 2 * pair_ids, 0, face_count - 1)]
        second = shuffled[jnp.clip(used_faces + 2 * pair_ids + 1, 0, face_count - 1)]
        pair_live = pair_ids < pair_count
        link_table = link_table.at[jnp.where(pair_live, first_face, face_count)].set(second, mode='drop')
        link_table = link_table.at[jnp.where(pair_live, second, face_count)].set(first_face, mode='drop')
        return (link_table, send_list)
    link_table, send_list = jax.vmap(per_device)(device_keys, block_counts, wall_counts)
    link_global = link_table.reshape(N_DOM, 4, E_DEV).transpose(1, 0, 2).reshape(4, N_DOM * E_DEV)
    return (link_global.astype(jnp.int32), send_list.reshape(N_DOM * blocks, CAP).astype(jnp.int32))


def draw_normals(key, part):
    first_key, second_key = jax.random.split(key)
    height = jax.random.uniform(first_key, (4, ELEMS), jnp.float32, -1.0, 1.0)
    angle = jax.random.uniform(second_key, (4, ELEMS), jnp.float32, -jnp.pi, jnp.pi)
    radius = jnp.sqrt(jnp.maximum(1.0 - height * height, 0.0))
    raw = jnp.stack([radius * jnp.cos(angle), radius * jnp.sin(angle), height]).astype(jnp.float32)
    face_count = 4 * E_DEV
    blocks = 2 * NBR_HALF
    link_global, send_list = make_links(key)
    codes = link_global.reshape(4, N_DOM, E_DEV).transpose(1, 0, 2).reshape(N_DOM, face_count)
    table = send_list.reshape(N_DOM, blocks, CAP)
    offsets = jnp.array([peer_shift(j, NBR_HALF) for j in range(blocks)], dtype=jnp.int32)
    mirror = (blocks - 1 - jnp.arange(blocks)).astype(jnp.int32)
    device_ids = jnp.arange(N_DOM, dtype=jnp.int32)[:, None]
    local_ids = jnp.arange(face_count, dtype=jnp.int32)[None, :]
    remote = jnp.maximum(codes - face_count, 0)
    block_ids = (remote // CAP).astype(jnp.int32)
    slot_ids = (remote % CAP).astype(jnp.int32)
    peer_ids = jnp.clip(device_ids + offsets[block_ids], 0, N_DOM - 1).astype(jnp.int32)
    peer_face = jnp.maximum(table[peer_ids, mirror[block_ids], slot_ids], 0)
    is_remote = codes >= face_count
    partner = jnp.where(is_remote, peer_ids * face_count + peer_face, device_ids * face_count + jnp.maximum(codes, 0)).astype(jnp.int32)
    follower = jnp.where(is_remote, offsets[block_ids] > 0, (codes >= 0) & (local_ids > codes))
    flat = raw.reshape(3, 4, N_DOM, E_DEV).transpose(0, 2, 1, 3).reshape(3, N_DOM * face_count)
    matched = jnp.where(follower.reshape(-1)[None, :], -flat[:, partner.reshape(-1)], flat)
    return matched.reshape(3, N_DOM, 4, E_DEV).transpose(0, 2, 1, 3).reshape(3, 4, ELEMS).astype(jnp.float32)


def draw_neighbour(key, part):
    return make_links(key)[0]


def draw_send_faces(key, part):
    return make_links(key)[1]


def plant(values, rng, least, top_value):
    shape = values.shape
    spot = [jax.random.randint(jax.random.fold_in(rng, axis), (), 0, shape[axis]) for axis in range(len(shape))]
    values = values.at[tuple(spot)].set(least)
    longest = shape.index(max(shape))
    spot[longest] = (spot[longest] + 1) % shape[longest]
    return values.at[tuple(spot)].set(top_value)


def steps_of(rng, shape, cuts, least, largest):
    gain = 1.0
    for dim, shards_of in cuts:
        draws = jax.random.uniform(jax.random.fold_in(jax.random.fold_in(rng, 6), dim), (shards_of,), jnp.float32, least / len(cuts), largest / len(cuts))
        gain = gain * jnp.repeat(jnp.exp(draws), shape[dim] // shards_of).reshape((-1,) + (1,) * (len(shape) - 1 - dim))
    return gain


def noise(stream_key, extent, spread, most, cuts=(), kind=jnp.bfloat16):
    values = spread * jax.random.normal(stream_key, extent, jnp.float32)
    if cuts:
        values = values * steps_of(stream_key, extent, cuts, -0.22, 0.18)
    return jnp.clip(values, -most, most).astype(kind)


def setup_inputs(seed: int = 0) -> dict:
    streams_of = jax.random.split(jax.random.key(seed), 11)
    solution = noise(streams_of[0], (4, NODES, ELEMS), 1.0, 6.0, ((2, 128),), jnp.float32)
    register = noise(streams_of[1], (4, NODES, ELEMS), 0.5, 4.0, ((2, 128),), jnp.float32)
    geometry = noise(streams_of[2], (9, ELEMS), 1.0, 4.0, ((1, 128),), jnp.float32)
    normals = draw_normals(jax.random.fold_in(streams_of[10], 71), 0)
    face_scale = jnp.clip(jnp.exp(math.log(2.0) - 1.3862944 * jax.random.uniform(streams_of[4], (4, ELEMS), jnp.float32) ** steps_of(streams_of[4], (4, ELEMS), ((1, 128),), -0.2, 0.2)), 0.5, 2.0)
    impedance = jnp.clip(jnp.exp(jax.random.uniform(streams_of[5], (NMAT,), jnp.float32, math.log(0.2), math.log(5.0))), 0.2, 5.0)
    neighbour = draw_neighbour(jax.random.fold_in(streams_of[10], 71), 0)
    orientation = plant(jax.random.randint(streams_of[7], (4, ELEMS), 0, 3), jax.random.fold_in(streams_of[7], 1), 0, 2).astype(jnp.int32)
    wall_material = plant(jax.random.randint(streams_of[8], (4, ELEMS), 0, NMAT), jax.random.fold_in(streams_of[8], 1), 0, NMAT - 1).astype(jnp.int32)
    send_faces = draw_send_faces(jax.random.fold_in(streams_of[10], 71), 0)
    return dict(solution=solution, register=register, geometry=geometry, normals=normals, face_scale=face_scale, impedance=impedance, neighbour=neighbour, orientation=orientation, wall_material=wall_material, send_faces=send_faces)


section_decay = (-567301805773.0 / 1357537059087.0, -2404267990393.0 / 2016746695238.0)
section_weight = (1720146321549.0 / 2090206949498.0, 3134564353537.0 / 4481467310338.0)
time_step = 0.002


def mat_product(left, right):
    inner = len(right)
    return [[sum(left[i][k] * right[k][j] for k in range(inner)) for j in range(len(right[0]))] for i in range(len(left))]


def flipped(matrix):
    return [list(row) for row in zip(*matrix)]


def solve_rows(matrix, right):
    size = len(matrix)
    augmented = [list(matrix[i]) + list(right[i]) for i in range(size)]
    for column in range(size):
        pivot = max(range(column, size), key=lambda r: abs(augmented[r][column]))
        augmented[column], augmented[pivot] = augmented[pivot], augmented[column]
        leader = augmented[column][column]
        augmented[column] = [value / leader for value in augmented[column]]
        for other in range(size):
            if other != column:
                factor = augmented[other][column]
                if factor != 0.0:
                    augmented[other] = [a - factor * b for a, b in zip(augmented[other], augmented[column])]
    return [row[size:] for row in augmented]


def identity_rows(size):
    return [[1.0 if i == j else 0.0 for j in range(size)] for i in range(size)]


def dg_tables():
    lattice = [(i, j, k) for i in range(4) for j in range(4 - i) for k in range(4 - i - j)]
    coords = [(i / 3.0, j / 3.0, k / 3.0) for (i, j, k) in lattice]
    vander = [[x ** a * y ** b * z ** c for (a, b, c) in lattice] for (x, y, z) in coords]
    inverse = solve_rows(vander, identity_rows(20))
    gradient_rows = []
    for d in range(3):
        derived = []
        for point in coords:
            row = []
            for powers in lattice:
                if powers[d] == 0:
                    row.append(0.0)
                else:
                    lowered = [powers[0], powers[1], powers[2]]
                    lowered[d] = lowered[d] - 1
                    row.append(powers[d] * point[0] ** lowered[0] * point[1] ** lowered[1] * point[2] ** lowered[2])
            derived.append(row)
        gradient_rows.extend(mat_product(derived, inverse))
    mono_mass = [[math.factorial(a + p) * math.factorial(b + q) * math.factorial(c + r) / math.factorial(a + b + c + p + q + r + 3) for (p, q, r) in lattice] for (a, b, c) in lattice]
    mass_matrix = mat_product(mat_product(flipped(inverse), mono_mass), inverse)
    plane_points = [(a, b) for a in range(4) for b in range(4 - a)]
    face_coords = [(a / 3.0, b / 3.0) for (a, b) in plane_points]
    vander_face = [[x ** a * y ** b for (a, b) in plane_points] for (x, y) in face_coords]
    inverse_face = solve_rows(vander_face, identity_rows(10))
    mono_face = [[math.factorial(a + p) * math.factorial(b + q) / math.factorial(a + b + p + q + 2) for (p, q) in plane_points] for (a, b) in plane_points]
    face_mass = mat_product(mat_product(flipped(inverse_face), mono_face), inverse_face)
    position = {point: n for n, point in enumerate(lattice)}
    builders = [lambda a, b: (a, b, 0), lambda a, b: (a, 0, b), lambda a, b: (0, a, b), lambda a, b: (a, b, 3 - a - b)]
    face_nodes = [[position[builder(a, b)] for (a, b) in plane_points] for builder in builders]
    surface = [[0.0] * 40 for n in range(20)]
    for f in range(4):
        for n in range(10):
            for m in range(10):
                surface[face_nodes[f][n]][f * 10 + m] = face_mass[n][m]
    lift_matrix = solve_rows(mass_matrix, surface)
    rotations = []
    for t in range(3):
        mapping = []
        for (a, b) in plane_points:
            triple = (b, a, 3 - a - b)
            for s in range(t):
                triple = (triple[1], triple[2], triple[0])
            mapping.append(plane_points.index((triple[0], triple[1])))
        rotations.append(mapping)
    return gradient_rows, lift_matrix, jnp.array(face_nodes, dtype=jnp.int32), jnp.array(rotations, dtype=jnp.int32)


def peer_offsets(half_span):
    return [j - half_span if j < half_span else j - half_span + 1 for j in range(2 * half_span)]


def local_traces(solution, face_nodes):
    elem_count = solution.shape[2]
    picked = solution[:, face_nodes.reshape(-1), :].reshape(4, 4, 10, elem_count)
    return picked.transpose(0, 2, 1, 3).reshape(4, 10, 4 * elem_count)


def orient_values(values, orientation, rotations):
    first_pick = values[:, rotations[0], :]
    second = values[:, rotations[1], :]
    third_pick = values[:, rotations[2], :]
    return jnp.where(orientation == 0, first_pick, jnp.where(orientation == 1, second, third_pick))


def wall_reflection(materials, impedance):
    material_ids = jnp.arange(impedance.shape[0], dtype=jnp.int32)
    picked = jnp.sum(jnp.where(materials[None, :] == material_ids[:, None], impedance[:, None], jnp.float32(0.0)), axis=0)
    return (picked - 1.0) / (picked + 1.0)


def face_flux(inner_trace, outer_trace, wall_mask, normal_flat, scale_flat, reflect):
    press_in = inner_trace[0]
    press_out = outer_trace[0]
    normal_in = normal_flat[0] * inner_trace[1] + normal_flat[1] * inner_trace[2] + normal_flat[2] * inner_trace[3]
    normal_out = normal_flat[0] * outer_trace[1] + normal_flat[1] * outer_trace[2] + normal_flat[2] * outer_trace[3]
    jump_press = jnp.where(wall_mask, (1.0 - reflect) * press_in, press_in - press_out)
    jump_normal = jnp.where(wall_mask, (1.0 + reflect) * normal_in, normal_in - normal_out)
    flux_press = 0.5 * scale_flat * (jump_normal - jump_press)
    flux_stack = jnp.stack([flux_press, -normal_flat[0] * flux_press, -normal_flat[1] * flux_press, -normal_flat[2] * flux_press])
    incoming = press_in + normal_in
    wall_loss = 0.25 * scale_flat * (1.0 - reflect * reflect) * incoming * incoming
    return flux_stack, wall_loss


def material_sums(wall_loss, wall_mask, materials, material_count):
    per_face = jnp.where(wall_mask, jnp.sum(wall_loss, axis=0), jnp.float32(0.0))
    material_ids = jnp.arange(material_count, dtype=jnp.int32)
    return jnp.sum(jnp.where(materials[None, :] == material_ids[:, None], per_face[None, :], jnp.float32(0.0)), axis=1)


def assemble(solution, geometry, flux_stack, gradient_ops, lift_matrix):
    elem_count = solution.shape[2]
    gradients = jnp.einsum('km,fme->fke', gradient_ops, solution, precision=lax.Precision.HIGHEST).reshape(4, 3, 20, elem_count)
    metric = geometry.reshape(3, 3, elem_count)

    def physical_derivative(field_index, i):
        return metric[i, 0] * gradients[field_index, 0] + metric[i, 1] * gradients[field_index, 1] + metric[i, 2] * gradients[field_index, 2]

    flux_faces = flux_stack.reshape(4, 10, 4, elem_count).transpose(0, 2, 1, 3).reshape(4, 40, elem_count)
    lifted = jnp.einsum('nk,fke->fne', lift_matrix, flux_faces, precision=lax.Precision.HIGHEST)
    divergence = physical_derivative(1, 0) + physical_derivative(2, 1) + physical_derivative(3, 2)
    return jnp.stack([lifted[0] - divergence, lifted[1] - physical_derivative(0, 0), lifted[2] - physical_derivative(0, 1), lifted[3] - physical_derivative(0, 2)])


def split_devices(array):
    leading = array.shape[:-1]
    return jnp.moveaxis(array.reshape(leading + (N_DOM, E_DEV)), -2, 0)


def reference(solution, register, geometry, normals, face_scale, impedance, neighbour, orientation, wall_material, send_faces):
    grad_rows, lift_rows, face_nodes, rotations = dg_tables()
    gradient_ops = jnp.asarray(grad_rows, dtype=jnp.float32)
    lift_matrix = jnp.asarray(lift_rows, dtype=jnp.float32)
    face_count = 4 * E_DEV
    blocks = 2 * NBR_HALF
    offsets = jnp.array(peer_offsets(NBR_HALF), dtype=jnp.int32)
    mirror = (blocks - 1 - jnp.arange(blocks)).astype(jnp.int32)
    link_codes = split_devices(neighbour).reshape(N_DOM, face_count)
    send_table = send_faces.reshape(N_DOM, blocks, CAP)
    device_ids = jnp.arange(N_DOM, dtype=jnp.int32)[:, None]
    remote_code = jnp.maximum(link_codes - face_count, 0)
    block_ids = (remote_code // CAP).astype(jnp.int32)
    slot_ids = (remote_code % CAP).astype(jnp.int32)
    peer_ids = jnp.clip(device_ids + offsets[block_ids], 0, N_DOM - 1).astype(jnp.int32)
    peer_face = send_table[peer_ids, mirror[block_ids], slot_ids]
    global_index = jnp.where(link_codes >= face_count, peer_ids * face_count + peer_face, device_ids * face_count + jnp.maximum(link_codes, 0)).astype(jnp.int32)
    dev_geometry = split_devices(geometry)
    dev_normals = split_devices(normals).reshape(N_DOM, 3, face_count)
    dev_scale = split_devices(face_scale).reshape(N_DOM, face_count)
    dev_orient = split_devices(orientation).reshape(N_DOM, face_count)
    dev_material = split_devices(wall_material).reshape(N_DOM, face_count)
    absorbed = []
    for section_index in range(2):
        dev_solution = split_devices(solution)
        all_traces = jax.vmap(lambda x: local_traces(x, face_nodes))(dev_solution)
        trace_table = all_traces.transpose(1, 2, 0, 3).reshape(40, N_DOM * face_count)

        def per_device(inputs):
            one_solution, one_geometry, one_normals, one_scale, one_links, one_index, one_orient, one_material = inputs
            inner_trace = local_traces(one_solution, face_nodes)
            outer_trace = jnp.take(trace_table, one_index, axis=1).reshape(4, 10, face_count)
            outer_trace = orient_values(outer_trace, one_orient, rotations)
            wall_mask = one_links < 0
            reflect = wall_reflection(one_material, impedance)
            flux_stack, wall_loss = face_flux(inner_trace, outer_trace, wall_mask, one_normals, one_scale, reflect)
            rhs_local = assemble(one_solution, one_geometry, flux_stack, gradient_ops, lift_matrix)
            totals = material_sums(wall_loss, wall_mask, one_material, impedance.shape[0])
            return rhs_local, totals

        rhs_dev, totals = lax.map(per_device, (dev_solution, dev_geometry, dev_normals, dev_scale, link_codes, global_index, dev_orient, dev_material))
        rhs_all = jnp.moveaxis(rhs_dev, 0, 2).reshape(4, 20, N_DOM * E_DEV)
        absorbed.append(jnp.sum(totals, axis=0) * (NMAT / (N_DOM * E_DEV)))
        register = section_decay[section_index] * register + time_step * rhs_all
        solution = solution + section_weight[section_index] * register
    return solution, register, jnp.stack(absorbed)
```

```python
import functools
import math

import jax
import jax.numpy as jnp
import numpy as np
from jax import lax
from jax.experimental import pallas as pl
from jax.experimental.pallas import tpu as pltpu
from jax.sharding import PartitionSpec as P

NMAT = 16
NODES = 20
LANES = 128

section_decay = (-567301805773.0 / 1357537059087.0, -2404267990393.0 / 2016746695238.0)
section_weight = (1720146321549.0 / 2090206949498.0, 3134564353537.0 / 4481467310338.0)
time_step = 0.002


def mat_product(left, right):
    inner = len(right)
    return [
        [sum((left[i][k] * right[k][j] for k in range(inner))) for j in range(len(right[0]))]
        for i in range(len(left))
    ]


def flipped(matrix):
    return [list(row) for row in zip(*matrix)]


def solve_rows(matrix, right):
    size = len(matrix)
    augmented = [list(matrix[i]) + list(right[i]) for i in range(size)]
    for column in range(size):
        pivot = max(range(column, size), key=lambda r: abs(augmented[r][column]))
        augmented[column], augmented[pivot] = (augmented[pivot], augmented[column])
        leader = augmented[column][column]
        augmented[column] = [value / leader for value in augmented[column]]
        for other in range(size):
            if other != column:
                factor = augmented[other][column]
                if factor != 0.0:
                    augmented[other] = [
                        a - factor * b for a, b in zip(augmented[other], augmented[column])
                    ]
    return [row[size:] for row in augmented]


def identity_rows(size):
    return [[1.0 if i == j else 0.0 for j in range(size)] for i in range(size)]


def dg_tables():
    lattice = [(i, j, k) for i in range(4) for j in range(4 - i) for k in range(4 - i - j)]
    coords = [(i / 3.0, j / 3.0, k / 3.0) for i, j, k in lattice]
    vander = [[x**a * y**b * z**c for a, b, c in lattice] for x, y, z in coords]
    inverse = solve_rows(vander, identity_rows(20))
    gradient_rows = []
    for d in range(3):
        derived = []
        for point in coords:
            row = []
            for powers in lattice:
                if powers[d] == 0:
                    row.append(0.0)
                else:
                    lowered = [powers[0], powers[1], powers[2]]
                    lowered[d] = lowered[d] - 1
                    row.append(
                        powers[d]
                        * point[0] ** lowered[0]
                        * point[1] ** lowered[1]
                        * point[2] ** lowered[2]
                    )
            derived.append(row)
        gradient_rows.extend(mat_product(derived, inverse))
    mono_mass = [
        [
            math.factorial(a + p)
            * math.factorial(b + q)
            * math.factorial(c + r)
            / math.factorial(a + b + c + p + q + r + 3)
            for p, q, r in lattice
        ]
        for a, b, c in lattice
    ]
    mass_matrix = mat_product(mat_product(flipped(inverse), mono_mass), inverse)
    plane_points = [(a, b) for a in range(4) for b in range(4 - a)]
    face_coords = [(a / 3.0, b / 3.0) for a, b in plane_points]
    vander_face = [[x**a * y**b for a, b in plane_points] for x, y in face_coords]
    inverse_face = solve_rows(vander_face, identity_rows(10))
    mono_face = [
        [
            math.factorial(a + p) * math.factorial(b + q) / math.factorial(a + b + p + q + 2)
            for p, q in plane_points
        ]
        for a, b in plane_points
    ]
    face_mass = mat_product(mat_product(flipped(inverse_face), mono_face), inverse_face)
    position = {point: n for n, point in enumerate(lattice)}
    builders = [
        lambda a, b: (a, b, 0),
        lambda a, b: (a, 0, b),
        lambda a, b: (0, a, b),
        lambda a, b: (a, b, 3 - a - b),
    ]
    face_nodes = [[position[builder(a, b)] for a, b in plane_points] for builder in builders]
    surface = [[0.0] * 40 for n in range(20)]
    for f in range(4):
        for n in range(10):
            for m in range(10):
                surface[face_nodes[f][n]][f * 10 + m] = face_mass[n][m]
    lift_matrix = solve_rows(mass_matrix, surface)
    rotations = []
    for t in range(3):
        mapping = []
        for a, b in plane_points:
            triple = (b, a, 3 - a - b)
            for s in range(t):
                triple = (triple[1], triple[2], triple[0])
            mapping.append(plane_points.index((triple[0], triple[1])))
        rotations.append(mapping)
    return (gradient_rows, lift_matrix, face_nodes, rotations)


def peer_offsets(half_span):
    return [j - half_span if j < half_span else j - half_span + 1 for j in range(2 * half_span)]


VMEM = pl.BlockSpec(memory_space=pltpu.VMEM)
SMEM = pl.BlockSpec(memory_space=pltpu.SMEM)
F32 = jnp.float32
GRAD_ROWS, LIFT_ROWS, FACE_NODES, ROTATIONS = dg_tables()
TILES = [(0, 8), (8, 8), (16, 4)]


def lanes_of(c):
    return pl.ds(pl.multiple_of(c * LANES, LANES), LANES)


def rows_of(c):
    return pl.ds(pl.multiple_of(c * 8, 8), 8)


def lookup(row, lane_index):
    wide = jnp.broadcast_to(row, (8, LANES))
    return jnp.take_along_axis(wide, lane_index, axis=1, mode="promise_in_bounds")


def split_bf16(x):
    high = x.astype(jnp.bfloat16)
    low = (x - high.astype(F32)).astype(jnp.bfloat16)
    return high, low


def mm(a, b):
    return jnp.dot(a, b, preferred_element_type=F32)


def faces_to_rows(src, scratch, dst, convert):
    chunks = src.shape[1] // LANES
    for c in range(chunks):
        scratch[c * 8 : c * 8 + 4, :] = src[:, c * LANES : (c + 1) * LANES]
    for f in range(4):
        for part in range(chunks // 8):
            got = scratch[pl.ds(part * 64 + f, 8, stride=8), :]
            row = f * chunks + part * 8
            dst[row : row + 8, :] = convert(got)


def wave_tiles(fields, c, normals, face_acc, press_acc):
    for r, (_, size) in enumerate(TILES):
        press, vel = fields[0][r], [fields[i][r] for i in (1, 2, 3)]
        press_acc[r, pl.ds(pl.multiple_of(c * 8, 8), size), :] = press
        for f in range(4):
            wave = press
            for i in range(3):
                wave = wave + normals[i, f : f + 1, lanes_of(c)] * vel[i]
            face_acc[f, r, pl.ds(pl.multiple_of(c * 8, 8), size), :] = wave


def send_and_totals(chunks, section, face_acc, press_acc, link, refl, half_scale, mat, send_faces, totals_in, g, d, buf):
    losses, keys = [], []
    for f in range(4):
        for part in range(chunks // 8):
            row = f * chunks + part * 8
            squares = jnp.zeros((8, LANES), F32)
            for n in range(10):
                node = FACE_NODES[f][n]
                at = pl.ds(part * 64 + node % 8, 8, stride=8)
                wave = face_acc[f, node // 8, at, :]
                g[n, row : row + 8, :] = wave
                d[n, row : row + 8, :] = wave - 2.0 * press_acc[node // 8, at, :]
                squares = squares + wave * wave
            r = refl[row : row + 8, :]
            loss = 0.5 * half_scale[row : row + 8, :] * (1.0 - r * r) * squares
            losses.append(jnp.where(link[row : row + 8, :] < 0, loss, 0.0))
            keys.append(mat[row : row + 8, :])
    lane = lax.broadcasted_iota(jnp.int32, (1, LANES), 1)
    totals = totals_in
    for m in range(NMAT):
        total = jnp.zeros((8, LANES), F32)
        for loss, key in zip(losses, keys):
            total = total + jnp.where(key == m, loss, 0.0)
        one = jnp.sum(jnp.sum(total, axis=0, keepdims=True), axis=1, keepdims=True)
        totals = jnp.where(lane == section * NMAT + m, one, totals)

    sends = send_faces[...]
    low = sends & (LANES - 1)
    high = lax.shift_right_arithmetic(sends, 7)
    acc = [jnp.zeros((8, LANES), F32) for _ in range(10)]
    for h in range(4 * chunks):
        here = high == h
        for n in range(10):
            acc[n] = jnp.where(here, lookup(g[n, h : h + 1, :], low), acc[n])
    me = lax.axis_index("dom")
    count = buf.shape[0]

    def put(i, carry):
        buf[i, :, 10 * LANES : 11 * LANES] = totals
        return carry

    lax.fori_loop(0, count, put, 0, unroll=8)
    for j, offset in enumerate(peer_offsets(4)):
        there = me + offset

        @pl.when((there >= 0) & (there < count))
        def _():
            for n in range(10):
                buf[there, :, n * LANES : (n + 1) * LANES] = acc[n][j : j + 1, :]

    return totals


def first_kernel(sol, normals, neighbour, orientation, material, scale, impedance, send_faces, g, d, buf, link, orient, half_scale, refl, mat, totals, face_acc, press_acc, tmp, tmp_int):
    chunks = sol.shape[2] // LANES
    faces_to_rows(neighbour, tmp_int, link, lambda x: x)
    faces_to_rows(orientation, tmp_int, orient, lambda x: x)
    faces_to_rows(scale, tmp, half_scale, lambda x: 0.5 * x)
    faces_to_rows(material, tmp_int, mat, lambda x: x)
    for row in range(0, 4 * chunks, 8):
        key = mat[row : row + 8, :]
        picked = jnp.zeros((8, LANES), F32)
        for m in range(NMAT):
            picked = jnp.where(key == m, impedance[m], picked)
        refl[row : row + 8, :] = (picked - 1.0) / (picked + 1.0)

    def chunk(c, carry):
        fields = [[sol[i, at : at + size, lanes_of(c)] for at, size in TILES] for i in range(4)]
        wave_tiles(fields, c, normals, face_acc, press_acc)
        return carry

    lax.fori_loop(0, chunks, chunk, 0, unroll=2)
    totals[...] = send_and_totals(chunks, 0, face_acc, press_acc, link, refl, half_scale, mat, send_faces, jnp.zeros((1, LANES), F32), g, d, buf)


def local_kernel(decay, sol, reg, geometry, link, g, grad, out_g, out_reg):
    chunks = sol.shape[2] // LANES
    wide = 2 * LANES

    def volume(b, carry):
        at = pl.ds(pl.multiple_of(b * wide, wide), wide)
        vel = [sol[i, :, at] for i in (1, 2, 3)]
        press = split_bf16(sol[0, :, at])
        metric = [geometry[k : k + 1, at] for k in range(9)]
        div = None
        slopes = []
        for a in range(3):
            matrix = grad[a]
            flow = split_bf16(metric[a] * vel[0] + metric[3 + a] * vel[1] + metric[6 + a] * vel[2])
            term = mm(matrix, flow[0]) + mm(matrix, flow[1])
            div = term if div is None else div + term
            slopes.append(mm(matrix, press[0]) + mm(matrix, press[1]))
        out_reg[0, :, at] = decay * reg[0, :, at] - time_step * div
        for i in range(3):
            slope = metric[3 * i] * slopes[0] + metric[3 * i + 1] * slopes[1] + metric[3 * i + 2] * slopes[2]
            out_reg[1 + i, :, at] = decay * reg[1 + i, :, at] - time_step * slope
        return carry

    lax.fori_loop(0, chunks // 2, volume, 0)

    def group(j, carry):
        codes = link[rows_of(j), :]
        low = codes & (LANES - 1)
        high = lax.shift_right_arithmetic(codes, 7)
        acc = [jnp.zeros((8, LANES), F32) for _ in range(10)]
        for h in range(4 * chunks):
            here = high == h
            for n in range(10):
                acc[n] = jnp.where(here, lookup(g[n, h : h + 1, :], low), acc[n])
        for n in range(10):
            out_g[n, rows_of(j), :] = acc[n]
        return carry

    lax.fori_loop(0, 4 * chunks // 8, group, 0)


def finish(section, chunks, sol, normals, link, orient, half_scale, refl, g, d, outer, recv, reg_part, lift_high, lift_low, new_sol, new_reg, flux_acc, after):
    me = lax.axis_index("dom")
    count = recv.shape[0]
    local_faces = 4 * chunks
    peers = [jnp.clip(me + offset, 0, count - 1) for offset in peer_offsets(4)]
    for f in range(4):

        def group(part, carry, f=f):
            rows = pl.ds(pl.multiple_of(f * chunks + part * 8, 8), 8)
            codes = link[rows, :]
            low = codes & (LANES - 1)
            high = lax.shift_right_arithmetic(codes, 7)
            acc = [outer[n, rows, :] for n in range(10)]
            for j in range(8):
                here = high == local_faces + j
                for n in range(10):
                    row = recv[peers[j], :, n * LANES : (n + 1) * LANES]
                    acc[n] = jnp.where(here, lookup(row, low), acc[n])
            turn = orient[rows, :]
            wall = codes < 0
            r = refl[rows, :]
            scale = half_scale[rows, :]
            for n in range(10):
                a, b, c = (ROTATIONS[t][n] for t in range(3))
                turned = acc[a] if a == b == c else jnp.where(turn == 0, acc[a], jnp.where(turn == 1, acc[b], acc[c]))
                turned = jnp.where(wall, r * g[n, rows, :], turned)
                k = f * 10 + n
                at = pl.ds(part * 64 + k % 8, 8, stride=8)
                flux_acc[k // 8, at, :] = scale * (d[n, rows, :] + turned)
            return carry

        lax.fori_loop(0, chunks // 8, group, 0)

    weight = section_weight[section]

    def chunk(c, carry):
        at = lanes_of(c)
        flux = split_bf16(jnp.concatenate([flux_acc[k, rows_of(c), :] for k in range(5)], axis=0))
        lifted = mm(lift_high[...], flux[0]) + mm(lift_high[...], flux[1]) + mm(lift_low[...], flux[0])
        fields = [[], [], [], []]
        for start, size in TILES:
            pieces = [lifted[24 * f + start : 24 * f + start + size, :] for f in range(4)]
            for i in range(4):
                if i == 0:
                    total = pieces[0] + pieces[1] + pieces[2] + pieces[3]
                else:
                    total = None
                    for f in range(4):
                        term = normals[i - 1, f : f + 1, at] * pieces[f]
                        total = term if total is None else total + term
                    total = -total
                reg = reg_part[i, start : start + size, at] + time_step * total
                value = sol[i, start : start + size, at] + weight * reg
                new_reg[i, start : start + size, at] = reg
                new_sol[i, start : start + size, at] = value
                fields[i].append(value)
        after(c, fields)
        return carry

    lax.fori_loop(0, chunks, chunk, 0, unroll=2)


def middle_kernel(sol, normals, link, orient, half_scale, refl, mat, send_faces, g, d, outer, recv, reg_part, lift_high, lift_low, totals_in, new_sol, new_reg, new_g, new_d, buf, flux_acc, face_acc, press_acc):
    chunks = sol.shape[2] // LANES

    def after(c, fields):
        wave_tiles(fields, c, normals, face_acc, press_acc)

    finish(0, chunks, sol, normals, link, orient, half_scale, refl, g, d, outer, recv, reg_part, lift_high, lift_low, new_sol, new_reg, flux_acc, after)
    send_and_totals(chunks, 1, face_acc, press_acc, link, refl, half_scale, mat, send_faces, totals_in[...], new_g, new_d, buf)


def last_kernel(norm_factor, sol, normals, link, orient, half_scale, refl, g, d, outer, recv, reg_part, lift_high, lift_low, new_sol, new_reg, absorbed, flux_acc):
    chunks = sol.shape[2] // LANES
    finish(1, chunks, sol, normals, link, orient, half_scale, refl, g, d, outer, recv, reg_part, lift_high, lift_low, new_sol, new_reg, flux_acc, lambda c, fields: None)
    total = recv[0, :, 10 * LANES : 11 * LANES]
    for i in range(1, recv.shape[0]):
        total = total + recv[i, :, 10 * LANES : 11 * LANES]
    total = total * norm_factor
    absorbed[0:1, :] = total[:, 0:NMAT]
    absorbed[1:2, :] = total[:, NMAT : 2 * NMAT]


def local(solution, register, geometry, normals, face_scale, impedance, neighbour, orientation, wall_material, send_faces):
    elems = solution.shape[2]
    chunks = elems // LANES
    devices = lax.axis_size("dom")
    rows = 4 * chunks
    shape = jax.ShapeDtypeStruct
    lift = np.zeros((96, 40), np.float64)
    for f in range(4):
        for n in range(NODES):
            lift[24 * f + n, 10 * f : 10 * f + 10] = LIFT_ROWS[n][10 * f : 10 * f + 10]
    lift_high = lift.astype(jnp.bfloat16)
    lift_low = (lift - lift_high.astype(np.float64)).astype(jnp.bfloat16)
    lift_high, lift_low = jnp.asarray(lift_high), jnp.asarray(lift_low)
    grad = jnp.asarray(np.array(GRAD_ROWS).reshape(3, NODES, NODES), jnp.bfloat16)
    state = shape(solution.shape, F32)
    wave = shape((10, rows, LANES), F32)
    packet = shape((devices, 1, 11 * LANES), F32)
    plane = shape((rows, LANES), F32)
    plane_int = shape((rows, LANES), jnp.int32)
    line = shape((1, LANES), F32)
    face_scratch = pltpu.VMEM((4, 3, 8 * chunks, LANES), F32)
    press_scratch = pltpu.VMEM((3, 8 * chunks, LANES), F32)
    flux_scratch = pltpu.VMEM((5, 8 * chunks, LANES), F32)

    def call(body, args, specs, outs, scratch, name, flops=2_000_000):
        return pl.pallas_call(
            body,
            out_shape=outs,
            in_specs=specs,
            out_specs=jax.tree.map(lambda _: VMEM, outs),
            scratch_shapes=scratch,
            cost_estimate=pl.CostEstimate(flops=flops, bytes_accessed=4_000_000, transcendentals=0),
            name=name,
        )(*args)

    g, d, buf, link, orient, half_scale, refl, mat, totals = call(
        first_kernel,
        (solution, normals, neighbour, orientation, wall_material, face_scale, impedance, send_faces),
        [VMEM] * 6 + [SMEM, VMEM],
        (wave, wave, packet, plane_int, plane_int, plane, plane, plane_int, line),
        [face_scratch, press_scratch, pltpu.VMEM((8 * chunks, LANES), F32), pltpu.VMEM((8 * chunks, LANES), jnp.int32)],
        "first",
    )

    def inner(section, sol, reg, g):
        return call(
            functools.partial(local_kernel, section_decay[section]),
            (sol, reg, geometry, link, g, grad),
            [VMEM] * 6,
            (wave, state),
            [],
            "inner",
            20_000_000,
        )

    recv = lax.all_to_all(buf, "dom", 0, 0)
    outer, reg_part = inner(0, solution, register, g)
    sol, reg, g, d, buf = call(
        middle_kernel,
        (solution, normals, link, orient, half_scale, refl, mat, send_faces, g, d, outer, recv, reg_part, lift_high, lift_low, totals),
        [VMEM] * 16,
        (state, state, wave, wave, packet),
        [flux_scratch, face_scratch, press_scratch],
        "middle",
    )
    recv = lax.all_to_all(buf, "dom", 0, 0)
    outer, reg_part = inner(1, sol, reg, g)
    sol, reg, absorbed = call(
        functools.partial(last_kernel, NMAT / (devices * elems)),
        (sol, normals, link, orient, half_scale, refl, g, d, outer, recv, reg_part, lift_high, lift_low),
        [VMEM] * 13,
        (state, state, shape((2, NMAT), F32)),
        [flux_scratch],
        "last",
    )
    return sol, reg, absorbed


def solution(mesh):
    in_specs = (
        P(None, None, "dom"),
        P(None, None, "dom"),
        P(None, "dom"),
        P(None, None, "dom"),
        P(None, "dom"),
        P(),
        P(None, "dom"),
        P(None, "dom"),
        P(None, "dom"),
        P("dom", None),
    )
    out_specs = (P(None, None, "dom"), P(None, None, "dom"), P())
    return jax.shard_map(local, mesh=mesh, in_specs=in_specs, out_specs=out_specs, check_vma=False)
```

```python
import functools
import math

import jax
import jax.numpy as jnp
import numpy as np
from jax import lax
from jax.experimental import pallas as pl
from jax.experimental.pallas import tpu as pltpu
from jax.sharding import PartitionSpec as P

NMAT = 16
NODES = 20
LANES = 128

section_decay = (-567301805773.0 / 1357537059087.0, -2404267990393.0 / 2016746695238.0)
section_weight = (1720146321549.0 / 2090206949498.0, 3134564353537.0 / 4481467310338.0)
time_step = 0.002


def mat_product(left, right):
    inner = len(right)
    return [
        [sum((left[i][k] * right[k][j] for k in range(inner))) for j in range(len(right[0]))]
        for i in range(len(left))
    ]


def flipped(matrix):
    return [list(row) for row in zip(*matrix)]


def solve_rows(matrix, right):
    size = len(matrix)
    augmented = [list(matrix[i]) + list(right[i]) for i in range(size)]
    for column in range(size):
        pivot = max(range(column, size), key=lambda r: abs(augmented[r][column]))
        augmented[column], augmented[pivot] = (augmented[pivot], augmented[column])
        leader = augmented[column][column]
        augmented[column] = [value / leader for value in augmented[column]]
        for other in range(size):
            if other != column:
                factor = augmented[other][column]
                if factor != 0.0:
                    augmented[other] = [
                        a - factor * b for a, b in zip(augmented[other], augmented[column])
                    ]
    return [row[size:] for row in augmented]


def identity_rows(size):
    return [[1.0 if i == j else 0.0 for j in range(size)] for i in range(size)]


def dg_tables():
    lattice = [(i, j, k) for i in range(4) for j in range(4 - i) for k in range(4 - i - j)]
    coords = [(i / 3.0, j / 3.0, k / 3.0) for i, j, k in lattice]
    vander = [[x**a * y**b * z**c for a, b, c in lattice] for x, y, z in coords]
    inverse = solve_rows(vander, identity_rows(20))
    gradient_rows = []
    for d in range(3):
        derived = []
        for point in coords:
            row = []
            for powers in lattice:
                if powers[d] == 0:
                    row.append(0.0)
                else:
                    lowered = [powers[0], powers[1], powers[2]]
                    lowered[d] = lowered[d] - 1
                    row.append(
                        powers[d]
                        * point[0] ** lowered[0]
                        * point[1] ** lowered[1]
                        * point[2] ** lowered[2]
                    )
            derived.append(row)
        gradient_rows.extend(mat_product(derived, inverse))
    mono_mass = [
        [
            math.factorial(a + p)
            * math.factorial(b + q)
            * math.factorial(c + r)
            / math.factorial(a + b + c + p + q + r + 3)
            for p, q, r in lattice
        ]
        for a, b, c in lattice
    ]
    mass_matrix = mat_product(mat_product(flipped(inverse), mono_mass), inverse)
    plane_points = [(a, b) for a in range(4) for b in range(4 - a)]
    face_coords = [(a / 3.0, b / 3.0) for a, b in plane_points]
    vander_face = [[x**a * y**b for a, b in plane_points] for x, y in face_coords]
    inverse_face = solve_rows(vander_face, identity_rows(10))
    mono_face = [
        [
            math.factorial(a + p) * math.factorial(b + q) / math.factorial(a + b + p + q + 2)
            for p, q in plane_points
        ]
        for a, b in plane_points
    ]
    face_mass = mat_product(mat_product(flipped(inverse_face), mono_face), inverse_face)
    position = {point: n for n, point in enumerate(lattice)}
    builders = [
        lambda a, b: (a, b, 0),
        lambda a, b: (a, 0, b),
        lambda a, b: (0, a, b),
        lambda a, b: (a, b, 3 - a - b),
    ]
    face_nodes = [[position[builder(a, b)] for a, b in plane_points] for builder in builders]
    surface = [[0.0] * 40 for n in range(20)]
    for f in range(4):
        for n in range(10):
            for m in range(10):
                surface[face_nodes[f][n]][f * 10 + m] = face_mass[n][m]
    lift_matrix = solve_rows(mass_matrix, surface)
    rotations = []
    for t in range(3):
        mapping = []
        for a, b in plane_points:
            triple = (b, a, 3 - a - b)
            for s in range(t):
                triple = (triple[1], triple[2], triple[0])
            mapping.append(plane_points.index((triple[0], triple[1])))
        rotations.append(mapping)
    return (gradient_rows, lift_matrix, face_nodes, rotations)


def peer_offsets(half_span):
    return [j - half_span if j < half_span else j - half_span + 1 for j in range(2 * half_span)]


VMEM = pl.BlockSpec(memory_space=pltpu.VMEM)
SMEM = pl.BlockSpec(memory_space=pltpu.SMEM)
F32 = jnp.float32
GRAD_ROWS, LIFT_ROWS, FACE_NODES, ROTATIONS = dg_tables()
LIFT_CHUNKS = 4
GRANT = None
BYTES = 4_000_000
TILES = [(0, 8), (8, 8), (16, 4)]


def lanes_of(c):
    return pl.ds(pl.multiple_of(c * LANES, LANES), LANES)


def rows_of(c):
    return pl.ds(pl.multiple_of(c * 8, 8), 8)


def lookup(row, lane_index):
    wide = jnp.broadcast_to(row, (8, LANES))
    return jnp.take_along_axis(wide, lane_index, axis=1, mode="promise_in_bounds")


def split_bf16(x):
    high = x.astype(jnp.bfloat16)
    low = (x - high.astype(F32)).astype(jnp.bfloat16)
    return high, low


def mm(a, b):
    return jnp.dot(a, b, preferred_element_type=F32)


class Staged:
    def __init__(self, outside, held, sems, count_in):
        self.outside, self.held, self.sems, self.count_in = outside, held, sems, count_in

    def copy(self, k):
        pair = (self.outside[k], self.held[k]) if k < self.count_in else (self.held[k], self.outside[k])
        return pltpu.make_async_copy(pair[0], pair[1], self.sems.at[k])


def staged(body, count_in, count_out, skip):
    total = count_in + count_out
    kept = [k for k in range(total) if k not in skip]

    def kernel(*refs):
        outside = refs[:total]
        held = list(outside)
        for at, k in enumerate(kept):
            held[k] = refs[total + at]
        rest = refs[total + len(kept) : -1]
        stage = Staged(outside, held, refs[-1], count_in)
        for k in kept:
            if k < count_in:
                stage.copy(k).start()
        waited, sent = set(), set()

        def wait(*names):
            for k in names:
                if k not in waited:
                    waited.add(k)
                    stage.copy(k).wait()

        def emit(*names):
            for k in names:
                sent.add(count_in + k)
                stage.copy(count_in + k).start()

        body(wait, emit, *held, *rest)
        wait(*[k for k in kept if k < count_in])
        emit(*[k - count_in for k in kept if k >= count_in and k not in sent])
        for k in kept:
            if k >= count_in:
                stage.copy(k).wait()

    return kernel, kept


def faces_to_rows(src, scratch, dst, convert):
    chunks = src.shape[1] // LANES
    for c in range(chunks):
        scratch[c * 8 : c * 8 + 4, :] = src[:, c * LANES : (c + 1) * LANES]
    for f in range(4):
        for part in range(chunks // 8):
            got = scratch[pl.ds(part * 64 + f, 8, stride=8), :]
            row = f * chunks + part * 8
            dst[row : row + 8, :] = convert(got)


def spread(src, dst, chunks):
    def chunk(c, carry):
        for node in range(NODES):
            dst[pl.ds(c * 24 + node, 4, stride=chunks * 24), :] = src[node, :, lanes_of(c)]
        return carry

    lax.fori_loop(0, chunks, chunk, 0, unroll=2)


def collect(src, dst, chunks):
    def chunk(c, carry):
        for node in range(NODES):
            dst[node, :, lanes_of(c)] = src[pl.ds(c * 24 + node, 4, stride=chunks * 24), :]
        return carry

    lax.fori_loop(0, chunks, chunk, 0, unroll=2)


def state_rows(field, c, chunks, start, size):
    return pl.ds(pl.multiple_of((field * chunks + c) * 24 + start, 8), size)


def wave_tiles(fields, c, chunks, normals, waves):
    for r, (start, size) in enumerate(TILES):
        press, vel = fields[0][r], [fields[i][r] for i in (1, 2, 3)]
        for f in range(4):
            wave = press
            for i in range(3):
                wave = wave + normals[i, f : f + 1, lanes_of(c)] * vel[i]
            waves[state_rows(f, c, chunks, start, size), :] = wave


def at_face(ref, field, chunks, part, node):
    return ref[pl.ds((field * chunks + part * 8) * 24 + node, 8, stride=24), :]


def pack(chunks, waves, send_faces, g, outgoing, filled):
    for f in range(4):
        for part in range(chunks // 8):
            row = f * chunks + part * 8
            for n in range(10):
                g[n, row : row + 8, :] = at_face(waves, f, chunks, part, FACE_NODES[f][n])
    filled()
    sends = send_faces[...]
    low = sends & (LANES - 1)
    high = lax.shift_right_arithmetic(sends, 7)
    acc = [jnp.zeros((8, LANES), F32) for _ in range(10)]
    for h in range(4 * chunks):
        here = high == h
        for n in range(10):
            acc[n] = jnp.where(here, lookup(g[n, h : h + 1, :], low), acc[n])
    for n in range(10):
        for j in range(8):
            outgoing[j, :, n * LANES : (n + 1) * LANES] = acc[n][j : j + 1, :]


def each_peer(count, act):
    me = lax.axis_index("dom")
    for j, offset in enumerate(peer_offsets(4)):
        there = me + offset

        @pl.when((there >= 0) & (there < count))
        def _():
            act(j, there)


def post(outgoing, buf, sems):
    def copy(j, there):
        return pltpu.make_async_copy(outgoing.at[j], buf.at[there, :, pl.ds(0, 10 * LANES)], sems.at[j])

    each_peer(buf.shape[0], lambda j, there: copy(j, there).start())
    return lambda: each_peer(buf.shape[0], lambda j, there: copy(j, there).wait())


def collect_blocks(recv, incoming, sems):
    def copy(j, there):
        return pltpu.make_async_copy(recv.at[there, :, pl.ds(0, 10 * LANES)], incoming.at[j], sems.at[j])

    each_peer(recv.shape[0], lambda j, there: copy(j, there).start())
    return lambda: each_peer(recv.shape[0], lambda j, there: copy(j, there).wait())


def wall_losses(section, chunks, g, link, refl, half_scale, mat, totals):
    losses, keys = [], []
    for row in range(0, 4 * chunks, 8):
        rows = slice(row, row + 8)
        squares = jnp.zeros((8, LANES), F32)
        for n in range(10):
            wave = g[n, rows, :]
            squares = squares + wave * wave
        r = refl[rows, :]
        losses.append(jnp.where(link[rows, :] < 0, 0.5 * half_scale[rows, :] * (1.0 - r * r) * squares, 0.0))
        keys.append(mat[rows, :])
    lane = lax.broadcasted_iota(jnp.int32, (1, LANES), 1)
    for m in range(NMAT):
        total = jnp.zeros((8, LANES), F32)
        for loss, key in zip(losses, keys):
            total = total + jnp.where(key == m, loss, 0.0)
        one = jnp.sum(jnp.sum(total, axis=0, keepdims=True), axis=1, keepdims=True)
        totals = jnp.where(lane == section * NMAT + m, one, totals)
    return totals


def first_kernel(wait, emit, sol, normals, send_faces, state, g, buf, waves, outgoing, sems):
    chunks = sol.shape[2] // LANES
    wait(0)
    spread(sol, state, chunks)
    emit(0)
    wait(1)

    def chunk(c, carry):
        fields = [[state[state_rows(i, c, chunks, start, size), :] for start, size in TILES] for i in range(4)]
        wave_tiles(fields, c, chunks, normals, waves)
        return carry

    lax.fori_loop(0, chunks, chunk, 0, unroll=2)
    wait(2)
    pack(chunks, waves, send_faces, g, outgoing, lambda: emit(1))
    post(outgoing, buf, sems)()


def inside(decay, chunks, state, reg, geometry, link, g, grad, out_g, out_reg):
    def volume(b, carry):
        def pair(ref, field):
            return jnp.concatenate([ref[state_rows(field, 2 * b + k, chunks, 0, NODES), :] for k in (0, 1)], axis=1)

        at = pl.ds(pl.multiple_of(b * 2 * LANES, 2 * LANES), 2 * LANES)
        vel = [pair(state, i) for i in (1, 2, 3)]
        press = split_bf16(pair(state, 0))
        metric = [geometry[k : k + 1, at] for k in range(9)]
        div = None
        slopes = []
        for a in range(3):
            matrix = grad[a]
            flow = split_bf16(metric[a] * vel[0] + metric[3 + a] * vel[1] + metric[6 + a] * vel[2])
            term = mm(matrix, flow[0]) + mm(matrix, flow[1])
            div = term if div is None else div + term
            slopes.append(mm(matrix, press[0]) + mm(matrix, press[1]))
        results = [div]
        for i in range(3):
            results.append(metric[3 * i] * slopes[0] + metric[3 * i + 1] * slopes[1] + metric[3 * i + 2] * slopes[2])
        for i in range(4):
            for k in (0, 1):
                rows = state_rows(i, 2 * b + k, chunks, 0, NODES)
                out_reg[rows, :] = decay * reg[rows, :] - time_step * results[i][:, k * LANES : (k + 1) * LANES]
        return carry

    lax.fori_loop(0, chunks // 2, volume, 0)

    def group(j, carry):
        codes = link[rows_of(j), :]
        low = codes & (LANES - 1)
        high = lax.shift_right_arithmetic(codes, 7)
        acc = [jnp.zeros((8, LANES), F32) for _ in range(10)]
        for h in range(4 * chunks):
            here = high == h
            for n in range(10):
                acc[n] = jnp.where(here, lookup(g[n, h : h + 1, :], low), acc[n])
        for n in range(10):
            out_g[n, rows_of(j), :] = acc[n]
        return carry

    lax.fori_loop(0, 4 * chunks // 8, group, 0)


def inner_first_kernel(wait, emit, state, reg, geometry, g, grad, neighbour, orientation, material, scale, impedance, out_g, out_reg, link, orient, half_scale, refl, mat, totals, reg_rows, tmp, tmp_int):
    chunks = neighbour.shape[1] // LANES
    wait(*range(9))
    faces_to_rows(neighbour, tmp_int, link, lambda x: x)
    faces_to_rows(orientation, tmp_int, orient, lambda x: x)
    faces_to_rows(scale, tmp, half_scale, lambda x: 0.5 * x)
    faces_to_rows(material, tmp_int, mat, lambda x: x)
    for row in range(0, 4 * chunks, 8):
        key = mat[row : row + 8, :]
        picked = jnp.zeros((8, LANES), F32)
        for m in range(NMAT):
            picked = jnp.where(key == m, impedance[m], picked)
        refl[row : row + 8, :] = (picked - 1.0) / (picked + 1.0)
    totals[...] = wall_losses(0, chunks, g, link, refl, half_scale, mat, jnp.zeros((1, LANES), F32))
    spread(reg, reg_rows, chunks)
    inside(section_decay[0], chunks, state, reg_rows, geometry, link, g, grad, out_g, out_reg)


def inner_second_kernel(wait, emit, state, reg, geometry, g, grad, link, out_g, out_reg):
    wait(*range(6))
    inside(section_decay[1], geometry.shape[1] // LANES, state, reg, geometry, link, g, grad, out_g, out_reg)


def finish(section, chunks, state, normals, link, orient, half_scale, refl, g, outer, incoming, reg_part, lift_high, lift_low, new_state, new_reg, flux_acc, lift_acc, ready, after):
    local_faces = 4 * chunks
    for f in range(4):
        for part in range(chunks // 8):
            row = f * chunks + part * 8
            rows = slice(row, row + 8)
            codes = link[rows, :]
            low = codes & (LANES - 1)
            high = lax.shift_right_arithmetic(codes, 7)
            acc = [outer[n, rows, :] for n in range(10)]
            for j in range(8):
                here = high == local_faces + j
                for n in range(10):
                    got = incoming[j, :, n * LANES : (n + 1) * LANES]
                    acc[n] = jnp.where(here, lookup(got, low), acc[n])
            turn = orient[rows, :]
            wall = codes < 0
            r = refl[rows, :]
            scale = half_scale[rows, :]
            for n in range(10):
                a, b, c = (ROTATIONS[t][n] for t in range(3))
                turned = acc[a] if a == b == c else jnp.where(turn == 0, acc[a], jnp.where(turn == 1, acc[b], acc[c]))
                own = g[n, rows, :]
                turned = own + jnp.where(wall, r * own, turned)
                press = at_face(state, 0, chunks, part, FACE_NODES[f][n])
                k = f * 10 + n
                flux_acc[k // 8, pl.ds(part * 64 + k % 8, 8, stride=8), :] = scale * (turned - 2.0 * press)

    for c in range(0, chunks, LIFT_CHUNKS):
        flux = split_bf16(
            jnp.concatenate(
                [jnp.concatenate([flux_acc[k, (c + b) * 8 : (c + b) * 8 + 8, :] for b in range(LIFT_CHUNKS)], axis=1) for k in range(5)],
                axis=0,
            )
        )
        lifted = mm(lift_high[...], flux[0]) + mm(lift_high[...], flux[1]) + mm(lift_low[...], flux[0])
        for b in range(LIFT_CHUNKS):
            lift_acc[c + b, :, :] = lifted[:, b * LANES : (b + 1) * LANES]

    weight = section_weight[section]
    ready()

    def chunk(c, carry):
        at = lanes_of(c)
        fields = [[], [], [], []]
        for start, size in TILES:
            pieces = [lift_acc[c, 24 * f + start : 24 * f + start + size, :] for f in range(4)]
            for i in range(4):
                if i == 0:
                    total = time_step * ((pieces[0] + pieces[1]) + (pieces[2] + pieces[3]))
                else:
                    terms = [normals[i - 1, f : f + 1, at] * pieces[f] for f in range(4)]
                    total = -time_step * ((terms[0] + terms[1]) + (terms[2] + terms[3]))
                rows = state_rows(i, c, chunks, start, size)
                reg = reg_part[rows, :] + total
                value = state[rows, :] + weight * reg
                new_reg[rows, :] = reg
                new_state[rows, :] = value
                fields[i].append(value)
        after(c, fields)
        return carry

    lax.fori_loop(0, chunks, chunk, 0, unroll=4)


def middle_kernel(wait, emit, state, normals, link, orient, half_scale, refl, mat, send_faces, g, outer, recv, reg_part, lift_high, lift_low, totals_in, new_state, new_reg, new_g, buf, flux_acc, lift_acc, waves, outgoing, incoming, losses, sems):
    chunks = normals.shape[2] // LANES
    arrived = collect_blocks(recv, incoming, sems)
    wait(0, 2, 3, 4, 5, 8, 9, 12, 13)
    arrived()

    def after(c, fields):
        wave_tiles(fields, c, chunks, normals, waves)

    finish(0, chunks, state, normals, link, orient, half_scale, refl, g, outer, incoming, reg_part, lift_high, lift_low, new_state, new_reg, flux_acc, lift_acc, lambda: wait(1, 11), after)
    emit(0, 1)
    wait(6, 7, 14)
    pack(chunks, waves, send_faces, new_g, outgoing, lambda: emit(2))
    posted = post(outgoing, buf, sems)
    totals = wall_losses(1, chunks, new_g, link, refl, half_scale, mat, totals_in[...])
    losses[...] = jnp.broadcast_to(totals, losses.shape)
    copy = pltpu.make_async_copy(losses, buf.at[:, 0, pl.ds(10 * LANES, LANES)], sems.at[8])
    copy.start()
    posted()
    copy.wait()


def last_kernel(norm_factor, wait, emit, state, normals, link, orient, half_scale, refl, g, outer, recv, reg_part, lift_high, lift_low, new_sol, new_reg, absorbed, flux_acc, lift_acc, sol_rows, reg_rows, incoming, losses, sems):
    chunks = normals.shape[2] // LANES
    arrived = collect_blocks(recv, incoming, sems)
    copy = pltpu.make_async_copy(recv.at[:, 0, pl.ds(10 * LANES, LANES)], losses, sems.at[8])
    copy.start()
    wait(0, 2, 3, 4, 5, 6, 7, 10, 11)
    arrived()
    finish(1, chunks, state, normals, link, orient, half_scale, refl, g, outer, incoming, reg_part, lift_high, lift_low, sol_rows, reg_rows, flux_acc, lift_acc, lambda: wait(1, 9), lambda c, fields: None)
    collect(reg_rows, new_reg, chunks)
    emit(1)
    collect(sol_rows, new_sol, chunks)
    emit(0)
    copy.wait()
    total = jnp.sum(losses[...], axis=0, keepdims=True) * norm_factor
    absorbed[0:1, :] = total[:, 0:NMAT]
    absorbed[1:2, :] = total[:, NMAT : 2 * NMAT]


def local(solution, register, geometry, normals, face_scale, impedance, neighbour, orientation, wall_material, send_faces):
    elems = solution.shape[2]
    chunks = elems // LANES
    devices = lax.axis_size("dom")
    rows = 4 * chunks
    shape = jax.ShapeDtypeStruct
    lift = np.zeros((96, 40), np.float64)
    for f in range(4):
        for n in range(NODES):
            lift[24 * f + n, 10 * f : 10 * f + 10] = LIFT_ROWS[n][10 * f : 10 * f + 10]
    lift_high = lift.astype(jnp.bfloat16)
    lift_low = (lift - lift_high.astype(np.float64)).astype(jnp.bfloat16)
    lift_high, lift_low = jnp.asarray(lift_high), jnp.asarray(lift_low)
    grad = jnp.asarray(np.array(GRAD_ROWS).reshape(3, NODES, NODES), jnp.bfloat16)
    swapped = shape((NODES, 4, elems), F32)
    state_shape = shape((4 * chunks * 24, LANES), F32)
    wave = shape((10, rows, LANES), F32)
    plane = shape((rows, LANES), F32)
    plane_int = shape((rows, LANES), jnp.int32)
    line = shape((1, LANES), F32)
    state_scratch = pltpu.VMEM((4 * chunks * 24, LANES), F32)
    flux_scratch = pltpu.VMEM((5, 8 * chunks, LANES), F32)
    lift_scratch = pltpu.VMEM((chunks, 96, LANES), F32)

    def packet(parts):
        return shape((devices, 1, parts * LANES), F32)

    def call(body, args, outs, scratch, name, flops=2_000_000, skip=()):
        total = len(args) + len(outs)
        skip = set(skip) | {k for k, a in enumerate(args) if a.ndim == 1}
        kernel, kept = staged(body, len(args), len(outs), skip)
        arrays = [*args, *outs]
        return pl.pallas_call(
            kernel,
            out_shape=outs,
            in_specs=[SMEM if a.ndim == 1 else pl.BlockSpec(memory_space=pl.ANY) for a in args],
            out_specs=tuple(pl.BlockSpec(memory_space=pl.ANY) for _ in outs),
            scratch_shapes=[pltpu.VMEM(arrays[k].shape, arrays[k].dtype) for k in kept]
            + scratch
            + [pltpu.SemaphoreType.DMA((total,))],
            compiler_params=pltpu.CompilerParams(vmem_limit_bytes=GRANT),
            cost_estimate=pl.CostEstimate(flops=flops, bytes_accessed=BYTES, transcendentals=0),
            name=name,
        )(*args)

    blocks = pltpu.VMEM((8, 1, 10 * LANES), F32)
    all_losses = pltpu.VMEM((devices, LANES), F32)
    sems = pltpu.SemaphoreType.DMA((9,))
    turned = solution.transpose(1, 0, 2)
    state, g, buf = call(first_kernel, (turned, normals, send_faces), (state_shape, wave, packet(10)), [state_scratch, blocks, sems], "first", skip=(5,))
    recv = pltpu.with_memory_space_constraint(lax.all_to_all(buf, "dom", 0, 0), pltpu.HBM)
    outer, reg_part, link, orient, half_scale, refl, mat, totals = call(
        inner_first_kernel,
        (state, register.transpose(1, 0, 2), geometry, g, grad, neighbour, orientation, wall_material, face_scale, impedance),
        (wave, state_shape, plane_int, plane_int, plane, plane, plane_int, line),
        [state_scratch, pltpu.VMEM((8 * chunks, LANES), F32), pltpu.VMEM((8 * chunks, LANES), jnp.int32)],
        "inner",
        20_000_000,
    )
    state, reg, g, buf = call(
        middle_kernel,
        (state, normals, link, orient, half_scale, refl, mat, send_faces, g, outer, recv, reg_part, lift_high, lift_low, totals),
        (state_shape, state_shape, wave, packet(11)),
        [flux_scratch, lift_scratch, state_scratch, blocks, blocks, all_losses, sems],
        "middle",
        skip=(10, 18),
    )
    recv = pltpu.with_memory_space_constraint(lax.all_to_all(buf, "dom", 0, 0), pltpu.HBM)
    outer, reg_part = call(
        inner_second_kernel, (state, reg, geometry, g, grad, link), (wave, state_shape), [], "inner_again", 20_000_000
    )
    sol, reg, absorbed = call(
        functools.partial(last_kernel, NMAT / (devices * elems)),
        (state, normals, link, orient, half_scale, refl, g, outer, recv, reg_part, lift_high, lift_low),
        (swapped, swapped, shape((2, NMAT), F32)),
        [flux_scratch, lift_scratch, state_scratch, state_scratch, blocks, all_losses, sems],
        "last",
        skip=(8,),
    )
    return sol.transpose(1, 0, 2), reg.transpose(1, 0, 2), absorbed


def solution(mesh):
    in_specs = (
        P(None, None, "dom"),
        P(None, None, "dom"),
        P(None, "dom"),
        P(None, None, "dom"),
        P(None, "dom"),
        P(),
        P(None, "dom"),
        P(None, "dom"),
        P(None, "dom"),
        P("dom", None),
    )
    out_specs = (P(None, None, "dom"), P(None, None, "dom"), P())
    return jax.shard_map(local, mesh=mesh, in_specs=in_specs, out_specs=out_specs, check_vma=False)
```

```python
import functools
import math

import jax
import jax.numpy as jnp
import numpy as np
from jax import lax
from jax.experimental import pallas as pl
from jax.experimental.pallas import tpu as pltpu
from jax.sharding import PartitionSpec as P

NMAT = 16
NODES = 20
LANES = 128

section_decay = (-567301805773.0 / 1357537059087.0, -2404267990393.0 / 2016746695238.0)
section_weight = (1720146321549.0 / 2090206949498.0, 3134564353537.0 / 4481467310338.0)
time_step = 0.002


def mat_product(left, right):
    inner = len(right)
    return [
        [sum((left[i][k] * right[k][j] for k in range(inner))) for j in range(len(right[0]))]
        for i in range(len(left))
    ]


def flipped(matrix):
    return [list(row) for row in zip(*matrix)]


def solve_rows(matrix, right):
    size = len(matrix)
    augmented = [list(matrix[i]) + list(right[i]) for i in range(size)]
    for column in range(size):
        pivot = max(range(column, size), key=lambda r: abs(augmented[r][column]))
        augmented[column], augmented[pivot] = (augmented[pivot], augmented[column])
        leader = augmented[column][column]
        augmented[column] = [value / leader for value in augmented[column]]
        for other in range(size):
            if other != column:
                factor = augmented[other][column]
                if factor != 0.0:
                    augmented[other] = [
                        a - factor * b for a, b in zip(augmented[other], augmented[column])
                    ]
    return [row[size:] for row in augmented]


def identity_rows(size):
    return [[1.0 if i == j else 0.0 for j in range(size)] for i in range(size)]


def dg_tables():
    lattice = [(i, j, k) for i in range(4) for j in range(4 - i) for k in range(4 - i - j)]
    coords = [(i / 3.0, j / 3.0, k / 3.0) for i, j, k in lattice]
    vander = [[x**a * y**b * z**c for a, b, c in lattice] for x, y, z in coords]
    inverse = solve_rows(vander, identity_rows(20))
    gradient_rows = []
    for d in range(3):
        derived = []
        for point in coords:
            row = []
            for powers in lattice:
                if powers[d] == 0:
                    row.append(0.0)
                else:
                    lowered = [powers[0], powers[1], powers[2]]
                    lowered[d] = lowered[d] - 1
                    row.append(
                        powers[d]
                        * point[0] ** lowered[0]
                        * point[1] ** lowered[1]
                        * point[2] ** lowered[2]
                    )
            derived.append(row)
        gradient_rows.extend(mat_product(derived, inverse))
    mono_mass = [
        [
            math.factorial(a + p)
            * math.factorial(b + q)
            * math.factorial(c + r)
            / math.factorial(a + b + c + p + q + r + 3)
            for p, q, r in lattice
        ]
        for a, b, c in lattice
    ]
    mass_matrix = mat_product(mat_product(flipped(inverse), mono_mass), inverse)
    plane_points = [(a, b) for a in range(4) for b in range(4 - a)]
    face_coords = [(a / 3.0, b / 3.0) for a, b in plane_points]
    vander_face = [[x**a * y**b for a, b in plane_points] for x, y in face_coords]
    inverse_face = solve_rows(vander_face, identity_rows(10))
    mono_face = [
        [
            math.factorial(a + p) * math.factorial(b + q) / math.factorial(a + b + p + q + 2)
            for p, q in plane_points
        ]
        for a, b in plane_points
    ]
    face_mass = mat_product(mat_product(flipped(inverse_face), mono_face), inverse_face)
    position = {point: n for n, point in enumerate(lattice)}
    builders = [
        lambda a, b: (a, b, 0),
        lambda a, b: (a, 0, b),
        lambda a, b: (0, a, b),
        lambda a, b: (a, b, 3 - a - b),
    ]
    face_nodes = [[position[builder(a, b)] for a, b in plane_points] for builder in builders]
    surface = [[0.0] * 40 for n in range(20)]
    for f in range(4):
        for n in range(10):
            for m in range(10):
                surface[face_nodes[f][n]][f * 10 + m] = face_mass[n][m]
    lift_matrix = solve_rows(mass_matrix, surface)
    rotations = []
    for t in range(3):
        mapping = []
        for a, b in plane_points:
            triple = (b, a, 3 - a - b)
            for s in range(t):
                triple = (triple[1], triple[2], triple[0])
            mapping.append(plane_points.index((triple[0], triple[1])))
        rotations.append(mapping)
    return (gradient_rows, lift_matrix, face_nodes, rotations)


def peer_offsets(half_span):
    return [j - half_span if j < half_span else j - half_span + 1 for j in range(2 * half_span)]


VMEM = pl.BlockSpec(memory_space=pltpu.VMEM)
SMEM = pl.BlockSpec(memory_space=pltpu.SMEM)
F32 = jnp.float32
GRAD_ROWS, LIFT_ROWS, FACE_NODES, ROTATIONS = dg_tables()
LIFT_CHUNKS = 4
GRANT = None
GRANTED = ('middle', 'last')
BYTES = 4_000_000
TILES = [(0, 8), (8, 8), (16, 4)]


def lanes_of(c):
    return pl.ds(pl.multiple_of(c * LANES, LANES), LANES)


def rows_of(c):
    return pl.ds(pl.multiple_of(c * 8, 8), 8)


def lookup(row, lane_index):
    wide = jnp.broadcast_to(row, (8, LANES))
    return jnp.take_along_axis(wide, lane_index, axis=1, mode="promise_in_bounds")


def split_bf16(x):
    high = x.astype(jnp.bfloat16)
    low = (x - high.astype(F32)).astype(jnp.bfloat16)
    return high, low


def mm(a, b):
    return jnp.dot(a, b, preferred_element_type=F32)


class Staged:
    def __init__(self, outside, held, sems, count_in):
        self.outside, self.held, self.sems, self.count_in = outside, held, sems, count_in

    def copy(self, k):
        pair = (self.outside[k], self.held[k]) if k < self.count_in else (self.held[k], self.outside[k])
        return pltpu.make_async_copy(pair[0], pair[1], self.sems.at[k])


def staged(body, count_in, count_out, skip):
    total = count_in + count_out
    kept = [k for k in range(total) if k not in skip]

    def kernel(*refs):
        outside = refs[:total]
        held = list(outside)
        for at, k in enumerate(kept):
            held[k] = refs[total + at]
        rest = refs[total + len(kept) : -1]
        stage = Staged(outside, held, refs[-1], count_in)
        order = sorted((k for k in kept if k < count_in), key=lambda k: math.prod(held[k].shape))
        waited, sent = set(), set()

        def wait(*names):
            for k in names:
                if k not in waited:
                    waited.add(k)
                    stage.copy(k).wait()

        def emit(*names):
            for k in names:
                sent.add(count_in + k)
                stage.copy(count_in + k).start()

        def begin():
            for k in order:
                stage.copy(k).start()

        wait.begin = begin
        body(wait, emit, *held, *rest)
        wait(*[k for k in kept if k < count_in])
        emit(*[k - count_in for k in kept if k >= count_in and k not in sent])
        for k in kept:
            if k >= count_in:
                stage.copy(k).wait()

    return kernel, kept


def faces_to_rows(src, scratch, dst, convert):
    chunks = src.shape[1] // LANES
    for c in range(chunks):
        scratch[c * 8 : c * 8 + 4, :] = src[:, c * LANES : (c + 1) * LANES]
    for f in range(4):
        for part in range(chunks // 8):
            got = scratch[pl.ds(part * 64 + f, 8, stride=8), :]
            row = f * chunks + part * 8
            dst[row : row + 8, :] = convert(got)


def spread(src, dst, chunks, start=0, stop=None):
    def chunk(c, carry):
        for node in range(NODES):
            dst[pl.ds(c * 24 + node, 4, stride=chunks * 24), :] = src[node, :, lanes_of(c)]
        return carry

    lax.fori_loop(start, chunks if stop is None else stop, chunk, 0, unroll=4)


def collect(src, dst, chunks, start, stop):
    for c in range(start, stop):
        for node in range(NODES):
            dst[node, :, c * LANES : (c + 1) * LANES] = src[pl.ds(c * 24 + node, 4, stride=chunks * 24), :]


def state_rows(field, c, chunks, start, size):
    return pl.ds(pl.multiple_of((field * chunks + c) * 24 + start, 8), size)


def wave_tiles(fields, c, chunks, normals, waves):
    for r, (start, size) in enumerate(TILES):
        press, vel = fields[0][r], [fields[i][r] for i in (1, 2, 3)]
        for f in range(4):
            wave = press
            for i in range(3):
                wave = wave + normals[i, f : f + 1, lanes_of(c)] * vel[i]
            waves[state_rows(f, c, chunks, start, size), :] = wave


def at_face(ref, field, chunks, part, node):
    return ref[pl.ds((field * chunks + part * 8) * 24 + node, 8, stride=24), :]


def pack(chunks, waves, send_faces, g, outgoing, filled):
    for f in range(4):
        for part in range(chunks // 8):
            row = f * chunks + part * 8
            for n in range(10):
                g[n, row : row + 8, :] = at_face(waves, f, chunks, part, FACE_NODES[f][n])
    filled()
    sends = send_faces[...]
    low = sends & (LANES - 1)
    high = lax.shift_right_arithmetic(sends, 7)
    acc = [jnp.zeros((8, LANES), F32) for _ in range(10)]
    for h in range(4 * chunks):
        here = high == h
        for n in range(10):
            acc[n] = jnp.where(here, lookup(g[n, h : h + 1, :], low), acc[n])
    for n in range(10):
        for j in range(8):
            outgoing[j, :, n * LANES : (n + 1) * LANES] = acc[n][j : j + 1, :]


def each_peer(count, act):
    me = lax.axis_index("dom")
    for j, offset in enumerate(peer_offsets(4)):
        there = me + offset

        @pl.when((there >= 0) & (there < count))
        def _():
            act(j, there)


def post(outgoing, buf, sems):
    def copy(j, there):
        return pltpu.make_async_copy(outgoing.at[j], buf.at[there, :, pl.ds(0, 10 * LANES)], sems.at[j])

    each_peer(buf.shape[0], lambda j, there: copy(j, there).start())
    return lambda: each_peer(buf.shape[0], lambda j, there: copy(j, there).wait())


def collect_blocks(recv, incoming, sems):
    def copy(j, there):
        return pltpu.make_async_copy(recv.at[there, :, pl.ds(0, 10 * LANES)], incoming.at[j], sems.at[j])

    each_peer(recv.shape[0], lambda j, there: copy(j, there).start())
    return lambda: each_peer(recv.shape[0], lambda j, there: copy(j, there).wait())


def wall_losses(section, chunks, g, link, refl, half_scale, mat, totals):
    losses, keys = [], []
    for row in range(0, 4 * chunks, 8):
        rows = slice(row, row + 8)
        squares = jnp.zeros((8, LANES), F32)
        for n in range(10):
            wave = g[n, rows, :]
            squares = squares + wave * wave
        r = refl[rows, :]
        losses.append(jnp.where(link[rows, :] < 0, 0.5 * half_scale[rows, :] * (1.0 - r * r) * squares, 0.0))
        keys.append(mat[rows, :])
    lane = lax.broadcasted_iota(jnp.int32, (1, LANES), 1)
    for m in range(NMAT):
        total = jnp.zeros((8, LANES), F32)
        for loss, key in zip(losses, keys):
            total = total + jnp.where(key == m, loss, 0.0)
        one = jnp.sum(jnp.sum(total, axis=0, keepdims=True), axis=1, keepdims=True)
        totals = jnp.where(lane == section * NMAT + m, one, totals)
    return totals


def first_kernel(wait, emit, sol_in, normals, send_faces, state, g, buf, waves, sol, outgoing, sems):
    chunks = sol.shape[2] // LANES
    part = chunks // 4
    copies = []
    for q in range(4):
        at = pl.ds(q * part * LANES, part * LANES)
        copies.append(pltpu.make_async_copy(sol_in.at[:, :, at], sol.at[:, :, at], sems.at[q]))
        copies[-1].start()
    wait.begin()

    def chunk(c, carry):
        fields = [[state[state_rows(i, c, chunks, start, size), :] for start, size in TILES] for i in range(4)]
        wave_tiles(fields, c, chunks, normals, waves)
        return carry

    wait(1)
    for q in range(4):
        copies[q].wait()
        spread(sol, state, chunks, q * part, (q + 1) * part)
        lax.fori_loop(q * part, (q + 1) * part, chunk, 0, unroll=2)
    emit(0)
    wait(2)
    pack(chunks, waves, send_faces, g, outgoing, lambda: emit(1))
    post(outgoing, buf, sems)()


def inside(decay, chunks, state, reg, geometry, link, refl, half_scale, g, grad, out_g, out_reg, out_base, prepare, finished):
    def volume(b, carry):
        def pair(ref, field):
            return jnp.concatenate([ref[state_rows(field, 2 * b + k, chunks, 0, NODES), :] for k in (0, 1)], axis=1)

        at = pl.ds(pl.multiple_of(b * 2 * LANES, 2 * LANES), 2 * LANES)
        vel = [pair(state, i) for i in (1, 2, 3)]
        press = split_bf16(pair(state, 0))
        metric = [geometry[k : k + 1, at] for k in range(9)]
        div = None
        slopes = []
        for a in range(3):
            matrix = grad[a]
            flow = split_bf16(metric[a] * vel[0] + metric[3 + a] * vel[1] + metric[6 + a] * vel[2])
            term = mm(matrix, flow[0]) + mm(matrix, flow[1])
            div = term if div is None else div + term
            slopes.append(mm(matrix, press[0]) + mm(matrix, press[1]))
        results = [div]
        for i in range(3):
            results.append(metric[3 * i] * slopes[0] + metric[3 * i + 1] * slopes[1] + metric[3 * i + 2] * slopes[2])
        for i in range(4):
            for k in (0, 1):
                rows = state_rows(i, 2 * b + k, chunks, 0, NODES)
                out_reg[rows, :] = decay * reg[rows, :] - time_step * results[i][:, k * LANES : (k + 1) * LANES]
        return carry

    def group(j, carry):
        codes = link[rows_of(j), :]
        low = codes & (LANES - 1)
        high = lax.shift_right_arithmetic(codes, 7)
        acc = [jnp.zeros((8, LANES), F32) for _ in range(10)]
        for h in range(4 * chunks):
            here = high == h
            for n in range(10):
                acc[n] = jnp.where(here, lookup(g[n, h : h + 1, :], low), acc[n])
        for n in range(10):
            out_g[n, rows_of(j), :] = acc[n]
        return carry

    lax.fori_loop(0, chunks // 4, group, 0)
    prepare()
    for f in range(4):
        for part in range(chunks // 8):
            row = f * chunks + part * 8
            rows = slice(row, row + 8)
            mirror = jnp.where(link[rows, :] < 0, 1.0 + refl[rows, :], 1.0)
            for n in range(10):
                press = at_face(state, 0, chunks, part, FACE_NODES[f][n])
                out_base[n, rows, :] = half_scale[rows, :] * (mirror * g[n, rows, :] - 2.0 * press)
    lax.fori_loop(0, chunks // 2, volume, 0)
    finished()
    lax.fori_loop(chunks // 4, chunks // 2, group, 0)


def inner_first_kernel(wait, emit, state, reg, geometry, g, grad, neighbour, orientation, material, scale, impedance, out_g, out_reg, out_base, link, orient, half_scale, refl, mat, totals, reg_rows, tmp, tmp_int):
    chunks = neighbour.shape[1] // LANES
    wait.begin()
    wait(5, 3)
    faces_to_rows(neighbour, tmp_int, link, lambda x: x)
    emit(3)

    def prepare():
        wait(6, 7, 8)
        faces_to_rows(orientation, tmp_int, orient, lambda x: x)
        faces_to_rows(scale, tmp, half_scale, lambda x: 0.5 * x)
        faces_to_rows(material, tmp_int, mat, lambda x: x)
        emit(4, 5, 7)
        for row in range(0, 4 * chunks, 8):
            key = mat[row : row + 8, :]
            picked = jnp.zeros((8, LANES), F32)
            for m in range(NMAT):
                picked = jnp.where(key == m, impedance[m], picked)
            refl[row : row + 8, :] = (picked - 1.0) / (picked + 1.0)
        emit(6)
        totals[...] = wall_losses(0, chunks, g, link, refl, half_scale, mat, jnp.zeros((1, LANES), F32))
        emit(8)
        wait(1)
        spread(reg, reg_rows, chunks)
        wait(0, 2, 4)

    inside(section_decay[0], chunks, state, reg_rows, geometry, link, refl, half_scale, g, grad, out_g, out_reg, out_base, prepare, lambda: emit(1, 2))


def inner_second_kernel(wait, emit, state, reg, geometry, g, grad, link, refl, half_scale, out_g, out_reg, out_base):
    wait.begin()
    wait(3, 5)
    inside(section_decay[1], geometry.shape[1] // LANES, state, reg, geometry, link, refl, half_scale, g, grad, out_g, out_reg, out_base, lambda: wait(0, 1, 2, 4, 6, 7), lambda: emit(1, 2))


def finish(section, chunks, state, normals, link, orient, half_scale, base, outer, incoming, reg_part, lift_high, lift_low, new_state, new_reg, flux_acc, lift_acc, ready, after, quarter=None):
    local_faces = 4 * chunks
    for f in range(4):
        for part in range(chunks // 8):
            row = f * chunks + part * 8
            rows = slice(row, row + 8)
            codes = link[rows, :]
            low = codes & (LANES - 1)
            high = lax.shift_right_arithmetic(codes, 7)
            acc = [outer[n, rows, :] for n in range(10)]
            for j in range(8):
                here = high == local_faces + j
                for n in range(10):
                    got = incoming[j, :, n * LANES : (n + 1) * LANES]
                    acc[n] = jnp.where(here, lookup(got, low), acc[n])
            turn = orient[rows, :]
            wall = codes < 0
            scale = half_scale[rows, :]
            for n in range(10):
                a, b, c = (ROTATIONS[t][n] for t in range(3))
                turned = acc[a] if a == b == c else jnp.where(turn == 0, acc[a], jnp.where(turn == 1, acc[b], acc[c]))
                k = f * 10 + n
                flux_acc[k // 8, pl.ds(part * 64 + k % 8, 8, stride=8), :] = base[n, rows, :] + jnp.where(wall, 0.0, scale * turned)

    for c in range(0, chunks, LIFT_CHUNKS):
        flux = split_bf16(
            jnp.concatenate(
                [jnp.concatenate([flux_acc[k, (c + b) * 8 : (c + b) * 8 + 8, :] for b in range(LIFT_CHUNKS)], axis=1) for k in range(5)],
                axis=0,
            )
        )
        lifted = mm(lift_high[...], flux[0]) + mm(lift_high[...], flux[1]) + mm(lift_low[...], flux[0])
        for b in range(LIFT_CHUNKS):
            lift_acc[c + b, :, :] = lifted[:, b * LANES : (b + 1) * LANES]

    weight = section_weight[section]
    ready()

    def chunk(c, carry):
        at = lanes_of(c)
        fields = [[], [], [], []]
        for start, size in TILES:
            pieces = [lift_acc[c, 24 * f + start : 24 * f + start + size, :] for f in range(4)]
            for i in range(4):
                if i == 0:
                    total = time_step * ((pieces[0] + pieces[1]) + (pieces[2] + pieces[3]))
                else:
                    terms = [normals[i - 1, f : f + 1, at] * pieces[f] for f in range(4)]
                    total = -time_step * ((terms[0] + terms[1]) + (terms[2] + terms[3]))
                rows = state_rows(i, c, chunks, start, size)
                reg = reg_part[rows, :] + total
                value = state[rows, :] + weight * reg
                new_reg[rows, :] = reg
                new_state[rows, :] = value
                fields[i].append(value)
        after(c, fields)
        return carry

    if quarter is None:
        lax.fori_loop(0, chunks, chunk, 0, unroll=4)
    else:
        for q in range(4):
            lax.fori_loop(q * chunks // 4, (q + 1) * chunks // 4, chunk, 0, unroll=True)
            quarter(q)


def middle_kernel(wait, emit, state, normals, link, orient, half_scale, refl, mat, send_faces, base, outer, recv, reg_part, lift_high, lift_low, totals_in, new_state, new_reg, new_g, buf, flux_acc, lift_acc, waves, outgoing, incoming, losses, sems):
    chunks = normals.shape[2] // LANES
    arrived = collect_blocks(recv, incoming, sems)
    wait.begin()
    wait(2, 3, 4, 8, 9, 12, 13)
    arrived()

    def after(c, fields):
        wave_tiles(fields, c, chunks, normals, waves)

    finish(0, chunks, state, normals, link, orient, half_scale, base, outer, incoming, reg_part, lift_high, lift_low, new_state, new_reg, flux_acc, lift_acc, lambda: wait(0, 1, 11), after)
    emit(0, 1)
    wait(5, 6, 7, 14)
    copy = pltpu.make_async_copy(losses, buf.at[:, 0, pl.ds(10 * LANES, LANES)], sems.at[8])

    def filled():
        emit(2)
        totals = wall_losses(1, chunks, new_g, link, refl, half_scale, mat, totals_in[...])
        losses[...] = jnp.broadcast_to(totals, losses.shape)
        copy.start()

    pack(chunks, waves, send_faces, new_g, outgoing, filled)
    posted = post(outgoing, buf, sems)
    posted()
    copy.wait()


def last_kernel(norm_factor, wait, emit, state, normals, link, orient, half_scale, base, outer, recv, reg_part, lift_high, lift_low, out_sol, out_reg, absorbed, flux_acc, lift_acc, sol_rows, reg_rows, new_sol, new_reg, incoming, losses, sems):
    chunks = normals.shape[2] // LANES
    arrived = collect_blocks(recv, incoming, sems)
    copy = pltpu.make_async_copy(recv.at[:, 0, pl.ds(10 * LANES, LANES)], losses, sems.at[8])
    copy.start()
    wait.begin()
    wait(2, 3, 4, 5, 6, 9, 10)
    arrived()
    copies = []

    def quarter(q):
        part = chunks // 4
        at = pl.ds(q * part * LANES, part * LANES)
        for k, (src, held, dst) in enumerate(((sol_rows, new_sol, out_sol), (reg_rows, new_reg, out_reg))):
            collect(src, held, chunks, q * part, (q + 1) * part)
            copies.append(pltpu.make_async_copy(held.at[:, :, at], dst.at[:, :, at], sems.at[9 + 2 * q + k]))
            copies[-1].start()

    finish(1, chunks, state, normals, link, orient, half_scale, base, outer, incoming, reg_part, lift_high, lift_low, sol_rows, reg_rows, flux_acc, lift_acc, lambda: wait(0, 1, 8), lambda c, fields: None, quarter)
    copy.wait()
    total = jnp.sum(losses[...], axis=0, keepdims=True) * norm_factor
    absorbed[0:1, :] = total[:, 0:NMAT]
    absorbed[1:2, :] = total[:, NMAT : 2 * NMAT]
    emit(2)
    for each in copies:
        each.wait()


def local(solution, register, geometry, normals, face_scale, impedance, neighbour, orientation, wall_material, send_faces):
    elems = solution.shape[2]
    chunks = elems // LANES
    devices = lax.axis_size("dom")
    rows = 4 * chunks
    shape = jax.ShapeDtypeStruct
    lift = np.zeros((96, 40), np.float64)
    for f in range(4):
        for n in range(NODES):
            lift[24 * f + n, 10 * f : 10 * f + 10] = LIFT_ROWS[n][10 * f : 10 * f + 10]
    lift_high = lift.astype(jnp.bfloat16)
    lift_low = (lift - lift_high.astype(np.float64)).astype(jnp.bfloat16)
    lift_high, lift_low = jnp.asarray(lift_high), jnp.asarray(lift_low)
    grad = jnp.asarray(np.array(GRAD_ROWS).reshape(3, NODES, NODES), jnp.bfloat16)
    swapped = shape((NODES, 4, elems), F32)
    state_shape = shape((4 * chunks * 24, LANES), F32)
    wave = shape((10, rows, LANES), F32)
    plane = shape((rows, LANES), F32)
    plane_int = shape((rows, LANES), jnp.int32)
    line = shape((1, LANES), F32)
    state_scratch = pltpu.VMEM((4 * chunks * 24, LANES), F32)
    flux_scratch = pltpu.VMEM((5, 8 * chunks, LANES), F32)
    lift_scratch = pltpu.VMEM((chunks, 96, LANES), F32)

    def packet(parts):
        return shape((devices, 1, parts * LANES), F32)

    def call(body, args, outs, scratch, name, flops=2_000_000, skip=()):
        total = len(args) + len(outs)
        skip = set(skip) | {k for k, a in enumerate(args) if a.ndim == 1}
        kernel, kept = staged(body, len(args), len(outs), skip)
        arrays = [*args, *outs]
        return pl.pallas_call(
            kernel,
            out_shape=outs,
            in_specs=[SMEM if a.ndim == 1 else pl.BlockSpec(memory_space=pl.ANY) for a in args],
            out_specs=tuple(pl.BlockSpec(memory_space=pl.ANY) for _ in outs),
            scratch_shapes=[pltpu.VMEM(arrays[k].shape, arrays[k].dtype) for k in kept]
            + scratch
            + [pltpu.SemaphoreType.DMA((total,))],
            compiler_params=pltpu.CompilerParams(vmem_limit_bytes=GRANT if name in GRANTED else None),
            cost_estimate=pl.CostEstimate(flops=flops, bytes_accessed=BYTES, transcendentals=0),
            name=name,
        )(*args)

    blocks = pltpu.VMEM((8, 1, 10 * LANES), F32)
    all_losses = pltpu.VMEM((devices, LANES), F32)
    sems = pltpu.SemaphoreType.DMA((9,))
    turned = solution.transpose(1, 0, 2)
    state, g, buf = call(first_kernel, (turned, normals, send_faces), (state_shape, wave, packet(10)), [state_scratch, pltpu.VMEM(swapped.shape, F32), blocks, sems], "first", skip=(0, 5))
    recv = lax.all_to_all(buf, "dom", 0, 0)
    outer, reg_part, base, link, orient, half_scale, refl, mat, totals = call(
        inner_first_kernel,
        (state, register.transpose(1, 0, 2), geometry, g, grad, neighbour, orientation, wall_material, face_scale, impedance),
        (wave, state_shape, wave, plane_int, plane_int, plane, plane, plane_int, line),
        [state_scratch, pltpu.VMEM((8 * chunks, LANES), F32), pltpu.VMEM((8 * chunks, LANES), jnp.int32)],
        "inner",
        20_000_000,
    )
    state, reg, g, buf = call(
        middle_kernel,
        (state, normals, link, orient, half_scale, refl, mat, send_faces, base, outer, recv, reg_part, lift_high, lift_low, totals),
        (state_shape, state_shape, wave, packet(11)),
        [flux_scratch, lift_scratch, state_scratch, blocks, blocks, all_losses, sems],
        "middle",
        skip=(10, 18),
    )
    recv = lax.all_to_all(buf, "dom", 0, 0)
    outer, reg_part, base = call(
        inner_second_kernel, (state, reg, geometry, g, grad, link, refl, half_scale), (wave, state_shape, wave), [], "inner_again", 20_000_000
    )
    sol, reg, absorbed = call(
        functools.partial(last_kernel, NMAT / (devices * elems)),
        (state, normals, link, orient, half_scale, base, outer, recv, reg_part, lift_high, lift_low),
        (swapped, swapped, shape((2, NMAT), F32)),
        [flux_scratch, lift_scratch, state_scratch, state_scratch]
        + [pltpu.VMEM(swapped.shape, F32)] * 2
        + [blocks, all_losses, pltpu.SemaphoreType.DMA((17,))],
        "last",
        skip=(7, 11, 12),
    )
    return sol.transpose(1, 0, 2), reg.transpose(1, 0, 2), absorbed


def solution(mesh):
    in_specs = (
        P(None, None, "dom"),
        P(None, None, "dom"),
        P(None, "dom"),
        P(None, None, "dom"),
        P(None, "dom"),
        P(),
        P(None, "dom"),
        P(None, "dom"),
        P(None, "dom"),
        P("dom", None),
    )
    out_specs = (P(None, None, "dom"), P(None, None, "dom"), P())
    return jax.shard_map(local, mesh=mesh, in_specs=in_specs, out_specs=out_specs, check_vma=False)
```

```python
import functools
import math

import jax
import jax.numpy as jnp
import numpy as np
from jax import lax
from jax.experimental import pallas as pl
from jax.experimental.pallas import tpu as pltpu
from jax.sharding import PartitionSpec as P

NMAT = 16
NODES = 20
LANES = 128

section_decay = (-567301805773.0 / 1357537059087.0, -2404267990393.0 / 2016746695238.0)
section_weight = (1720146321549.0 / 2090206949498.0, 3134564353537.0 / 4481467310338.0)
time_step = 0.002


def mat_product(left, right):
    inner = len(right)
    return [
        [sum((left[i][k] * right[k][j] for k in range(inner))) for j in range(len(right[0]))]
        for i in range(len(left))
    ]


def flipped(matrix):
    return [list(row) for row in zip(*matrix)]


def solve_rows(matrix, right):
    size = len(matrix)
    augmented = [list(matrix[i]) + list(right[i]) for i in range(size)]
    for column in range(size):
        pivot = max(range(column, size), key=lambda r: abs(augmented[r][column]))
        augmented[column], augmented[pivot] = (augmented[pivot], augmented[column])
        leader = augmented[column][column]
        augmented[column] = [value / leader for value in augmented[column]]
        for other in range(size):
            if other != column:
                factor = augmented[other][column]
                if factor != 0.0:
                    augmented[other] = [
                        a - factor * b for a, b in zip(augmented[other], augmented[column])
                    ]
    return [row[size:] for row in augmented]


def identity_rows(size):
    return [[1.0 if i == j else 0.0 for j in range(size)] for i in range(size)]


def dg_tables():
    lattice = [(i, j, k) for i in range(4) for j in range(4 - i) for k in range(4 - i - j)]
    coords = [(i / 3.0, j / 3.0, k / 3.0) for i, j, k in lattice]
    vander = [[x**a * y**b * z**c for a, b, c in lattice] for x, y, z in coords]
    inverse = solve_rows(vander, identity_rows(20))
    gradient_rows = []
    for d in range(3):
        derived = []
        for point in coords:
            row = []
            for powers in lattice:
                if powers[d] == 0:
                    row.append(0.0)
                else:
                    lowered = [powers[0], powers[1], powers[2]]
                    lowered[d] = lowered[d] - 1
                    row.append(
                        powers[d]
                        * point[0] ** lowered[0]
                        * point[1] ** lowered[1]
                        * point[2] ** lowered[2]
                    )
            derived.append(row)
        gradient_rows.extend(mat_product(derived, inverse))
    mono_mass = [
        [
            math.factorial(a + p)
            * math.factorial(b + q)
            * math.factorial(c + r)
            / math.factorial(a + b + c + p + q + r + 3)
            for p, q, r in lattice
        ]
        for a, b, c in lattice
    ]
    mass_matrix = mat_product(mat_product(flipped(inverse), mono_mass), inverse)
    plane_points = [(a, b) for a in range(4) for b in range(4 - a)]
    face_coords = [(a / 3.0, b / 3.0) for a, b in plane_points]
    vander_face = [[x**a * y**b for a, b in plane_points] for x, y in face_coords]
    inverse_face = solve_rows(vander_face, identity_rows(10))
    mono_face = [
        [
            math.factorial(a + p) * math.factorial(b + q) / math.factorial(a + b + p + q + 2)
            for p, q in plane_points
        ]
        for a, b in plane_points
    ]
    face_mass = mat_product(mat_product(flipped(inverse_face), mono_face), inverse_face)
    position = {point: n for n, point in enumerate(lattice)}
    builders = [
        lambda a, b: (a, b, 0),
        lambda a, b: (a, 0, b),
        lambda a, b: (0, a, b),
        lambda a, b: (a, b, 3 - a - b),
    ]
    face_nodes = [[position[builder(a, b)] for a, b in plane_points] for builder in builders]
    surface = [[0.0] * 40 for n in range(20)]
    for f in range(4):
        for n in range(10):
            for m in range(10):
                surface[face_nodes[f][n]][f * 10 + m] = face_mass[n][m]
    lift_matrix = solve_rows(mass_matrix, surface)
    rotations = []
    for t in range(3):
        mapping = []
        for a, b in plane_points:
            triple = (b, a, 3 - a - b)
            for s in range(t):
                triple = (triple[1], triple[2], triple[0])
            mapping.append(plane_points.index((triple[0], triple[1])))
        rotations.append(mapping)
    return (gradient_rows, lift_matrix, face_nodes, rotations)


def peer_offsets(half_span):
    return [j - half_span if j < half_span else j - half_span + 1 for j in range(2 * half_span)]


VMEM = pl.BlockSpec(memory_space=pltpu.VMEM)
SMEM = pl.BlockSpec(memory_space=pltpu.SMEM)
F32 = jnp.float32
GRAD_ROWS, LIFT_ROWS, FACE_NODES, ROTATIONS = dg_tables()
LIFT_CHUNKS = 4
GRANT = None
UNROLL = 8
GRANTED = ('middle', 'last')
BYTES = 4_000_000
TILES = [(0, 8), (8, 8), (16, 4)]


def lanes_of(c):
    return pl.ds(pl.multiple_of(c * LANES, LANES), LANES)


def rows_of(c):
    return pl.ds(pl.multiple_of(c * 8, 8), 8)


def lookup(row, lane_index):
    wide = jnp.broadcast_to(row, (8, LANES))
    return jnp.take_along_axis(wide, lane_index, axis=1, mode="promise_in_bounds")


def split_bf16(x):
    high = x.astype(jnp.bfloat16)
    low = (x - high.astype(F32)).astype(jnp.bfloat16)
    return high, low


def mm(a, b):
    return jnp.dot(a, b, preferred_element_type=F32)


class Staged:
    def __init__(self, outside, held, sems, count_in):
        self.outside, self.held, self.sems, self.count_in = outside, held, sems, count_in

    def copy(self, k):
        pair = (self.outside[k], self.held[k]) if k < self.count_in else (self.held[k], self.outside[k])
        return pltpu.make_async_copy(pair[0], pair[1], self.sems.at[k])


def staged(body, count_in, count_out, skip):
    total = count_in + count_out
    kept = [k for k in range(total) if k not in skip]

    def kernel(*refs):
        outside = refs[:total]
        held = list(outside)
        for at, k in enumerate(kept):
            held[k] = refs[total + at]
        rest = refs[total + len(kept) : -1]
        stage = Staged(outside, held, refs[-1], count_in)
        order = sorted((k for k in kept if k < count_in), key=lambda k: math.prod(held[k].shape))
        waited, sent = set(), set()

        def wait(*names):
            for k in names:
                if k not in waited:
                    waited.add(k)
                    stage.copy(k).wait()

        def emit(*names):
            for k in names:
                sent.add(count_in + k)
                stage.copy(count_in + k).start()

        def begin():
            for k in order:
                stage.copy(k).start()

        wait.begin = begin
        body(wait, emit, *held, *rest)
        wait(*[k for k in kept if k < count_in])
        emit(*[k - count_in for k in kept if k >= count_in and k not in sent])
        for k in kept:
            if k >= count_in:
                stage.copy(k).wait()

    return kernel, kept


def faces_to_rows(src, scratch, dst, convert):
    chunks = src.shape[1] // LANES
    for c in range(chunks):
        scratch[c * 8 : c * 8 + 4, :] = src[:, c * LANES : (c + 1) * LANES]
    for f in range(4):
        for part in range(chunks // 8):
            got = scratch[pl.ds(part * 64 + f, 8, stride=8), :]
            row = f * chunks + part * 8
            dst[row : row + 8, :] = convert(got)


def spread(src, dst, chunks, start=0, stop=None):
    def chunk(c, carry):
        for node in range(NODES):
            dst[pl.ds(c * 24 + node, 4, stride=chunks * 24), :] = src[node, :, lanes_of(c)]
        return carry

    lax.fori_loop(start, chunks if stop is None else stop, chunk, 0, unroll=4)


def collect(src, dst, chunks, start, stop):
    for c in range(start, stop):
        for node in range(NODES):
            dst[node, :, c * LANES : (c + 1) * LANES] = src[pl.ds(c * 24 + node, 4, stride=chunks * 24), :]


def state_rows(field, c, chunks, start, size):
    return pl.ds(pl.multiple_of((field * chunks + c) * 24 + start, 8), size)


def wave_tiles(fields, c, chunks, normals, waves):
    for r, (start, size) in enumerate(TILES):
        press, vel = fields[0][r], [fields[i][r] for i in (1, 2, 3)]
        for f in range(4):
            wave = press
            for i in range(3):
                wave = wave + normals[i, f : f + 1, lanes_of(c)] * vel[i]
            waves[state_rows(f, c, chunks, start, size), :] = wave


def at_face(ref, field, chunks, part, node):
    return ref[pl.ds((field * chunks + part * 8) * 24 + node, 8, stride=24), :]


def pack(chunks, waves, send_faces, g, outgoing, filled):
    for f in range(4):
        for part in range(chunks // 8):
            row = f * chunks + part * 8
            for n in range(10):
                g[n, row : row + 8, :] = at_face(waves, f, chunks, part, FACE_NODES[f][n])
    filled()
    sends = send_faces[...]
    low = sends & (LANES - 1)
    high = lax.shift_right_arithmetic(sends, 7)
    acc = [jnp.zeros((8, LANES), F32) for _ in range(10)]
    for h in range(4 * chunks):
        here = high == h
        for n in range(10):
            acc[n] = jnp.where(here, lookup(g[n, h : h + 1, :], low), acc[n])
    for n in range(10):
        for j in range(8):
            outgoing[j, :, n * LANES : (n + 1) * LANES] = acc[n][j : j + 1, :]


def each_peer(count, act):
    me = lax.axis_index("dom")
    for j, offset in enumerate(peer_offsets(4)):
        there = me + offset

        @pl.when((there >= 0) & (there < count))
        def _():
            act(j, there)


def post(outgoing, buf, sems):
    def copy(j, there):
        return pltpu.make_async_copy(outgoing.at[j], buf.at[there, :, pl.ds(0, 10 * LANES)], sems.at[j])

    each_peer(buf.shape[0], lambda j, there: copy(j, there).start())
    return lambda: each_peer(buf.shape[0], lambda j, there: copy(j, there).wait())


def collect_blocks(recv, incoming, sems):
    def copy(j, there):
        return pltpu.make_async_copy(recv.at[there, :, pl.ds(0, 10 * LANES)], incoming.at[j], sems.at[j])

    each_peer(recv.shape[0], lambda j, there: copy(j, there).start())
    return lambda: each_peer(recv.shape[0], lambda j, there: copy(j, there).wait())


def wall_losses(section, chunks, g, link, refl, half_scale, mat, totals):
    losses, keys = [], []
    for row in range(0, 4 * chunks, 8):
        rows = slice(row, row + 8)
        squares = jnp.zeros((8, LANES), F32)
        for n in range(10):
            wave = g[n, rows, :]
            squares = squares + wave * wave
        r = refl[rows, :]
        losses.append(jnp.where(link[rows, :] < 0, 0.5 * half_scale[rows, :] * (1.0 - r * r) * squares, 0.0))
        keys.append(mat[rows, :])
    lane = lax.broadcasted_iota(jnp.int32, (1, LANES), 1)
    for m in range(NMAT):
        total = jnp.zeros((8, LANES), F32)
        for loss, key in zip(losses, keys):
            total = total + jnp.where(key == m, loss, 0.0)
        one = jnp.sum(jnp.sum(total, axis=0, keepdims=True), axis=1, keepdims=True)
        totals = jnp.where(lane == section * NMAT + m, one, totals)
    return totals


def first_kernel(wait, emit, sol_in, normals, send_faces, state, g, buf, waves, sol, outgoing, sems):
    chunks = sol.shape[2] // LANES
    part = chunks // 4
    copies = []
    for q in range(4):
        at = pl.ds(q * part * LANES, part * LANES)
        copies.append(pltpu.make_async_copy(sol_in.at[:, :, at], sol.at[:, :, at], sems.at[q]))
        copies[-1].start()
    wait.begin()

    def chunk(c, carry):
        fields = [[state[state_rows(i, c, chunks, start, size), :] for start, size in TILES] for i in range(4)]
        wave_tiles(fields, c, chunks, normals, waves)
        return carry

    wait(1)
    for q in range(4):
        copies[q].wait()
        spread(sol, state, chunks, q * part, (q + 1) * part)
        lax.fori_loop(q * part, (q + 1) * part, chunk, 0, unroll=2)
    emit(0)
    wait(2)
    pack(chunks, waves, send_faces, g, outgoing, lambda: emit(1))
    post(outgoing, buf, sems)()


def inside(decay, chunks, state, reg, geometry, link, refl, half_scale, g, grad, out_g, out_reg, out_base, prepare, finished):
    def volume(b, carry):
        def pair(ref, field):
            return jnp.concatenate([ref[state_rows(field, 2 * b + k, chunks, 0, NODES), :] for k in (0, 1)], axis=1)

        at = pl.ds(pl.multiple_of(b * 2 * LANES, 2 * LANES), 2 * LANES)
        vel = [pair(state, i) for i in (1, 2, 3)]
        press = split_bf16(pair(state, 0))
        metric = [geometry[k : k + 1, at] for k in range(9)]
        div = None
        slopes = []
        for a in range(3):
            matrix = grad[a]
            flow = split_bf16(metric[a] * vel[0] + metric[3 + a] * vel[1] + metric[6 + a] * vel[2])
            term = mm(matrix, flow[0]) + mm(matrix, flow[1])
            div = term if div is None else div + term
            slopes.append(mm(matrix, press[0]) + mm(matrix, press[1]))
        results = [div]
        for i in range(3):
            results.append(metric[3 * i] * slopes[0] + metric[3 * i + 1] * slopes[1] + metric[3 * i + 2] * slopes[2])
        for i in range(4):
            for k in (0, 1):
                rows = state_rows(i, 2 * b + k, chunks, 0, NODES)
                out_reg[rows, :] = decay * reg[rows, :] - time_step * results[i][:, k * LANES : (k + 1) * LANES]
        return carry

    def group(j, carry):
        codes = link[rows_of(j), :]
        low = codes & (LANES - 1)
        high = lax.shift_right_arithmetic(codes, 7)
        acc = [jnp.zeros((8, LANES), F32) for _ in range(10)]
        for h in range(4 * chunks):
            here = high == h
            for n in range(10):
                acc[n] = jnp.where(here, lookup(g[n, h : h + 1, :], low), acc[n])
        for n in range(10):
            out_g[n, rows_of(j), :] = acc[n]
        return carry

    lax.fori_loop(0, chunks // 4, group, 0)
    prepare()
    for f in range(4):
        for part in range(chunks // 8):
            row = f * chunks + part * 8
            rows = slice(row, row + 8)
            mirror = jnp.where(link[rows, :] < 0, 1.0 + refl[rows, :], 1.0)
            for n in range(10):
                press = at_face(state, 0, chunks, part, FACE_NODES[f][n])
                out_base[n, rows, :] = half_scale[rows, :] * (mirror * g[n, rows, :] - 2.0 * press)
    lax.fori_loop(0, chunks // 2, volume, 0)
    finished()
    lax.fori_loop(chunks // 4, chunks // 2, group, 0)


def inner_first_kernel(wait, emit, state, reg, geometry, g, grad, neighbour, orientation, material, scale, impedance, out_g, out_reg, out_base, link, orient, half_scale, refl, mat, totals, reg_rows, tmp, tmp_int):
    chunks = neighbour.shape[1] // LANES
    wait.begin()
    wait(5, 3)
    faces_to_rows(neighbour, tmp_int, link, lambda x: x)
    emit(3)

    def prepare():
        wait(6, 7, 8)
        faces_to_rows(orientation, tmp_int, orient, lambda x: x)
        faces_to_rows(scale, tmp, half_scale, lambda x: 0.5 * x)
        faces_to_rows(material, tmp_int, mat, lambda x: x)
        emit(4, 5, 7)
        for row in range(0, 4 * chunks, 8):
            key = mat[row : row + 8, :]
            picked = jnp.zeros((8, LANES), F32)
            for m in range(NMAT):
                picked = jnp.where(key == m, impedance[m], picked)
            refl[row : row + 8, :] = (picked - 1.0) / (picked + 1.0)
        emit(6)
        totals[...] = wall_losses(0, chunks, g, link, refl, half_scale, mat, jnp.zeros((1, LANES), F32))
        emit(8)
        wait(1)
        spread(reg, reg_rows, chunks)
        wait(0, 2, 4)

    inside(section_decay[0], chunks, state, reg_rows, geometry, link, refl, half_scale, g, grad, out_g, out_reg, out_base, prepare, lambda: emit(1, 2))


def inner_second_kernel(wait, emit, state, reg, geometry, g, grad, link, refl, half_scale, out_g, out_reg, out_base):
    wait.begin()
    wait(3, 5)
    inside(section_decay[1], geometry.shape[1] // LANES, state, reg, geometry, link, refl, half_scale, g, grad, out_g, out_reg, out_base, lambda: wait(0, 1, 2, 4, 6, 7), lambda: emit(1, 2))


def finish(section, chunks, state, normals, link, orient, half_scale, base, outer, incoming, reg_part, lift_high, lift_low, new_state, new_reg, flux_acc, lift_acc, ready, after, quarter=None):
    local_faces = 4 * chunks
    for f in range(4):
        for part in range(chunks // 8):
            row = f * chunks + part * 8
            rows = slice(row, row + 8)
            codes = link[rows, :]
            low = codes & (LANES - 1)
            high = lax.shift_right_arithmetic(codes, 7)
            acc = [outer[n, rows, :] for n in range(10)]
            for j in range(8):
                here = high == local_faces + j
                for n in range(10):
                    got = incoming[j, :, n * LANES : (n + 1) * LANES]
                    acc[n] = jnp.where(here, lookup(got, low), acc[n])
            turn = orient[rows, :]
            wall = codes < 0
            scale = half_scale[rows, :]
            for n in range(10):
                a, b, c = (ROTATIONS[t][n] for t in range(3))
                turned = acc[a] if a == b == c else jnp.where(turn == 0, acc[a], jnp.where(turn == 1, acc[b], acc[c]))
                k = f * 10 + n
                flux_acc[k // 8, pl.ds(part * 64 + k % 8, 8, stride=8), :] = base[n, rows, :] + jnp.where(wall, 0.0, scale * turned)

    for c in range(0, chunks, LIFT_CHUNKS):
        flux = split_bf16(
            jnp.concatenate(
                [jnp.concatenate([flux_acc[k, (c + b) * 8 : (c + b) * 8 + 8, :] for b in range(LIFT_CHUNKS)], axis=1) for k in range(5)],
                axis=0,
            )
        )
        lifted = mm(lift_high[...], flux[0]) + mm(lift_high[...], flux[1]) + mm(lift_low[...], flux[0])
        for b in range(LIFT_CHUNKS):
            lift_acc[c + b, :, :] = lifted[:, b * LANES : (b + 1) * LANES]

    weight = section_weight[section]
    ready()

    def chunk(c, carry):
        at = lanes_of(c)
        fields = [[], [], [], []]
        for start, size in TILES:
            pieces = [lift_acc[c, 24 * f + start : 24 * f + start + size, :] for f in range(4)]
            for i in range(4):
                if i == 0:
                    total = time_step * ((pieces[0] + pieces[1]) + (pieces[2] + pieces[3]))
                else:
                    terms = [normals[i - 1, f : f + 1, at] * pieces[f] for f in range(4)]
                    total = -time_step * ((terms[0] + terms[1]) + (terms[2] + terms[3]))
                rows = state_rows(i, c, chunks, start, size)
                reg = reg_part[rows, :] + total
                value = state[rows, :] + weight * reg
                new_reg[rows, :] = reg
                new_state[rows, :] = value
                fields[i].append(value)
        after(c, fields)
        return carry

    if quarter is None:
        lax.fori_loop(0, chunks, chunk, 0, unroll=UNROLL)
    else:
        for q in range(4):
            lax.fori_loop(q * chunks // 4, (q + 1) * chunks // 4, chunk, 0, unroll=True)
            quarter(q)


def middle_kernel(wait, emit, state, normals, link, orient, half_scale, refl, mat, send_faces, base, outer, recv, reg_part, lift_high, lift_low, totals_in, new_state, new_reg, new_g, buf, flux_acc, lift_acc, waves, outgoing, incoming, losses, sems):
    chunks = normals.shape[2] // LANES
    arrived = collect_blocks(recv, incoming, sems)
    wait.begin()
    wait(2, 3, 4, 8, 9, 12, 13)
    arrived()

    def after(c, fields):
        wave_tiles(fields, c, chunks, normals, waves)

    finish(0, chunks, state, normals, link, orient, half_scale, base, outer, incoming, reg_part, lift_high, lift_low, new_state, new_reg, flux_acc, lift_acc, lambda: wait(0, 1, 11), after)
    emit(0, 1)
    wait(5, 6, 7, 14)
    copy = pltpu.make_async_copy(losses, buf.at[:, 0, pl.ds(10 * LANES, LANES)], sems.at[8])

    def filled():
        emit(2)
        totals = wall_losses(1, chunks, new_g, link, refl, half_scale, mat, totals_in[...])
        losses[...] = jnp.broadcast_to(totals, losses.shape)
        copy.start()

    pack(chunks, waves, send_faces, new_g, outgoing, filled)
    posted = post(outgoing, buf, sems)
    posted()
    copy.wait()


def last_kernel(norm_factor, wait, emit, state, normals, link, orient, half_scale, base, outer, recv, reg_part, lift_high, lift_low, out_sol, out_reg, absorbed, flux_acc, lift_acc, sol_rows, reg_rows, new_sol, new_reg, incoming, losses, sems):
    chunks = normals.shape[2] // LANES
    arrived = collect_blocks(recv, incoming, sems)
    copy = pltpu.make_async_copy(recv.at[:, 0, pl.ds(10 * LANES, LANES)], losses, sems.at[8])
    copy.start()
    wait.begin()
    wait(2, 3, 4, 5, 6, 9, 10)
    arrived()
    copies = []

    def quarter(q):
        part = chunks // 4
        at = pl.ds(q * part * LANES, part * LANES)
        for k, (src, held, dst) in enumerate(((sol_rows, new_sol, out_sol), (reg_rows, new_reg, out_reg))):
            collect(src, held, chunks, q * part, (q + 1) * part)
            copies.append(pltpu.make_async_copy(held.at[:, :, at], dst.at[:, :, at], sems.at[9 + 2 * q + k]))
            copies[-1].start()

    finish(1, chunks, state, normals, link, orient, half_scale, base, outer, incoming, reg_part, lift_high, lift_low, sol_rows, reg_rows, flux_acc, lift_acc, lambda: wait(0, 1, 8), lambda c, fields: None, quarter)
    copy.wait()
    total = jnp.sum(losses[...], axis=0, keepdims=True) * norm_factor
    absorbed[0:1, :] = total[:, 0:NMAT]
    absorbed[1:2, :] = total[:, NMAT : 2 * NMAT]
    emit(2)
    for each in copies:
        each.wait()


def local(solution, register, geometry, normals, face_scale, impedance, neighbour, orientation, wall_material, send_faces):
    elems = solution.shape[2]
    chunks = elems // LANES
    devices = lax.axis_size("dom")
    rows = 4 * chunks
    shape = jax.ShapeDtypeStruct
    lift = np.zeros((96, 40), np.float64)
    for f in range(4):
        for n in range(NODES):
            lift[24 * f + n, 10 * f : 10 * f + 10] = LIFT_ROWS[n][10 * f : 10 * f + 10]
    lift_high = lift.astype(jnp.bfloat16)
    lift_low = (lift - lift_high.astype(np.float64)).astype(jnp.bfloat16)
    lift_high, lift_low = jnp.asarray(lift_high), jnp.asarray(lift_low)
    grad = jnp.asarray(np.array(GRAD_ROWS).reshape(3, NODES, NODES), jnp.bfloat16)
    swapped = shape((NODES, 4, elems), F32)
    state_shape = shape((4 * chunks * 24, LANES), F32)
    wave = shape((10, rows, LANES), F32)
    plane = shape((rows, LANES), F32)
    plane_int = shape((rows, LANES), jnp.int32)
    line = shape((1, LANES), F32)
    state_scratch = pltpu.VMEM((4 * chunks * 24, LANES), F32)
    flux_scratch = pltpu.VMEM((5, 8 * chunks, LANES), F32)
    lift_scratch = pltpu.VMEM((chunks, 96, LANES), F32)

    def packet(parts):
        return shape((devices, 1, parts * LANES), F32)

    def call(body, args, outs, scratch, name, flops=2_000_000, skip=()):
        total = len(args) + len(outs)
        skip = set(skip) | {k for k, a in enumerate(args) if a.ndim == 1}
        kernel, kept = staged(body, len(args), len(outs), skip)
        arrays = [*args, *outs]
        return pl.pallas_call(
            kernel,
            out_shape=outs,
            in_specs=[SMEM if a.ndim == 1 else pl.BlockSpec(memory_space=pl.ANY) for a in args],
            out_specs=tuple(pl.BlockSpec(memory_space=pl.ANY) for _ in outs),
            scratch_shapes=[pltpu.VMEM(arrays[k].shape, arrays[k].dtype) for k in kept]
            + scratch
            + [pltpu.SemaphoreType.DMA((total,))],
            compiler_params=pltpu.CompilerParams(vmem_limit_bytes=GRANT if name in GRANTED else None),
            cost_estimate=pl.CostEstimate(flops=flops, bytes_accessed=BYTES, transcendentals=0),
            name=name,
        )(*args)

    blocks = pltpu.VMEM((8, 1, 10 * LANES), F32)
    all_losses = pltpu.VMEM((devices, LANES), F32)
    sems = pltpu.SemaphoreType.DMA((9,))
    turned = solution.transpose(1, 0, 2)
    state, g, buf = call(first_kernel, (turned, normals, send_faces), (state_shape, wave, packet(10)), [state_scratch, pltpu.VMEM(swapped.shape, F32), blocks, sems], "first", skip=(0, 5))
    recv = lax.all_to_all(buf, "dom", 0, 0)
    outer, reg_part, base, link, orient, half_scale, refl, mat, totals = call(
        inner_first_kernel,
        (state, register.transpose(1, 0, 2), geometry, g, grad, neighbour, orientation, wall_material, face_scale, impedance),
        (wave, state_shape, wave, plane_int, plane_int, plane, plane, plane_int, line),
        [state_scratch, pltpu.VMEM((8 * chunks, LANES), F32), pltpu.VMEM((8 * chunks, LANES), jnp.int32)],
        "inner",
        20_000_000,
    )
    state, reg, g, buf = call(
        middle_kernel,
        (state, normals, link, orient, half_scale, refl, mat, send_faces, base, outer, recv, reg_part, lift_high, lift_low, totals),
        (state_shape, state_shape, wave, packet(11)),
        [flux_scratch, lift_scratch, state_scratch, blocks, blocks, all_losses, sems],
        "middle",
        skip=(10, 18),
    )
    recv = lax.all_to_all(buf, "dom", 0, 0)
    outer, reg_part, base = call(
        inner_second_kernel, (state, reg, geometry, g, grad, link, refl, half_scale), (wave, state_shape, wave), [], "inner_again", 20_000_000
    )
    sol, reg, absorbed = call(
        functools.partial(last_kernel, NMAT / (devices * elems)),
        (state, normals, link, orient, half_scale, base, outer, recv, reg_part, lift_high, lift_low),
        (swapped, swapped, shape((2, NMAT), F32)),
        [flux_scratch, lift_scratch, state_scratch, state_scratch]
        + [pltpu.VMEM(swapped.shape, F32)] * 2
        + [blocks, all_losses, pltpu.SemaphoreType.DMA((17,))],
        "last",
        skip=(7, 11, 12),
    )
    return sol.transpose(1, 0, 2), reg.transpose(1, 0, 2), absorbed


def solution(mesh):
    in_specs = (
        P(None, None, "dom"),
        P(None, None, "dom"),
        P(None, "dom"),
        P(None, None, "dom"),
        P(None, "dom"),
        P(),
        P(None, "dom"),
        P(None, "dom"),
        P(None, "dom"),
        P("dom", None),
    )
    out_specs = (P(None, None, "dom"), P(None, None, "dom"), P())
    return jax.shard_map(local, mesh=mesh, in_specs=in_specs, out_specs=out_specs, check_vma=False)
```
